128 devices in a mesh: tiles: 64 (over y, z_hi, x, core), vec: 2 (over z_lo).
Axes of the slice: x: 4, y: 4, z: 4 (z_hi: 2, z_lo: 2; z = z_hi * 2 + z_lo), core: 2. Of those that a mesh axis runs over, the one named last changes fastest.
Arguments:
- omega: float32 [128, 4, 512, 128], P('vec', None, 'tiles'), may hold values from -24 to 24
- conductance: float32 [3, 4, 512, 128], P(None, None, 'tiles'), may hold values from 0.02 to 0.16
- wet: int32 [512, 128], P('tiles'), may hold values 0 or 1
- volume: float32 [512, 128], P('tiles'), may hold values from 0.3 to 27, as said below
- face_runs: int32 [64, 4], P('tiles'), may hold values from 0 to 128, as said below
Outputs:
- diffused: float32 [128, 4, 512, 128], P('vec', None, 'tiles')
- r_factor: float32 [128, 128], replicated
The draws below stay inside these ranges and needn't reach their ends.
Inputs may be any that keep to these rules, and one draw needn't show every extreme that they name: `face_runs`: tiles in tile row 0 have a closed lower row face and tiles in tile column 0 a closed lower column face (length 0); every other run lies within its face, covers at least half of it, and some tiles have fully open faces. Positive cell volume weights.
All inputs are finite; a program needn't handle non-finite values. No bound on the sum of `wet` on one device may be relied on, other than what follows from the above.
Results may differ from the reference program's by a relative error of at most 0.00005.
Values sent between devices are 32-bit elements; how exact they have to be, the bound alone decides.
A program may use at most 64 MiB of HBM per device.

```python
import math
import jax
import jax.numpy as jnp
from jax import lax

VECS = 128
TGY = 8
ITERS = 4
LEV = 4
TX = 8
TY = 128
TILES = 64
TGX = 8


def draw_omega(key, part):
    first, second = jax.random.split(jax.random.fold_in(key, 11), 2)
    shape = (VECS, LEV, TILES * TX, TY)
    common_shape = (1, LEV, TILES * TX, TY)
    own = jax.random.normal(first, shape, jnp.float32)
    common = jax.random.normal(second, common_shape, jnp.float32)
    values = jnp.clip((own + 0.5 * common) / math.sqrt(1.25), -8.0, 8.0)
    return values.astype(jnp.float32)


def draw_volume(key, part):
    tile_of_row = (jnp.arange(TILES * TX) // TX).astype(jnp.float32)
    ramp = 1.0 + 2.0 * tile_of_row / (TILES - 1)
    rough = jnp.exp(jax.random.uniform(jax.random.fold_in(key, 22), (TILES * TX, TY), jnp.float32, math.log(0.5), math.log(2.0)))
    values = ramp[:, None] * rough
    return values.astype(jnp.float32)


def draw_face_runs(key, part):
    first, second, third, fourth = jax.random.split(jax.random.fold_in(key, 31), 4)
    tile_ids = jnp.arange(TILES, dtype=jnp.int32)
    tile_row = tile_ids // TGY
    tile_col = tile_ids % TGY
    length_x = jax.random.randint(first, (TILES,), TY // 2, TY + 1, dtype=jnp.int32)
    length_x = jnp.where(tile_ids % 3 == 0, TY, length_x)
    length_x = jnp.where(tile_row == 0, 0, length_x)
    start_x = jax.random.randint(second, (TILES,), 0, 1 << 20, dtype=jnp.int32) % (TY - length_x + 1)
    length_y = jax.random.randint(third, (TILES,), TX // 2, TX + 1, dtype=jnp.int32)
    length_y = jnp.where(tile_ids % 3 == 1, TX, length_y)
    length_y = jnp.where(tile_col == 0, 0, length_y)
    start_y = jax.random.randint(fourth, (TILES,), 0, 1 << 20, dtype=jnp.int32) % (TX - length_y + 1)
    return jnp.stack([start_x, length_x, start_y, length_y], axis=1).astype(jnp.int32)


def place_ends(entries, own_key, low, high):
    index_at = [jax.random.randint(jax.random.fold_in(own_key, axis), (), 0, length) for axis, length in enumerate(entries.shape)]
    longest = entries.shape.index(max(entries.shape))
    neighbour = index_at[:longest] + [(index_at[longest] + 1) % entries.shape[longest]] + index_at[longest + 1:]
    return entries.at[tuple(index_at)].set(low).at[tuple(neighbour)].set(high)


def block_levels(key, shape, cuts, low, top_value):
    gain = 1.0
    for axis_at, parts in cuts:
        draws = jax.random.uniform(jax.random.fold_in(jax.random.fold_in(key, 6), axis_at), (parts,), jnp.float32, low / len(cuts), top_value / len(cuts))
        gain = gain * jnp.repeat(jnp.exp(draws), shape[axis_at] // parts).reshape((-1,) + (1,) * (len(shape) - 1 - axis_at))
    return gain


def setup_inputs(seed: int = 0) -> dict:
    splits = jax.random.split(jax.random.key(seed), 6)
    omega = draw_omega(jax.random.fold_in(splits[5], 71), 0)
    conductance = jnp.clip(jnp.exp(math.log(0.16) - 2.0794415 * jax.random.uniform(splits[1], (3, LEV, TILES * TX, TY), jnp.float32) ** block_levels(splits[1], (3, LEV, TILES * TX, TY), ((2, 64),), -0.2, 0.2)), 0.02, 0.16)
    wet = place_ends((jax.random.randint(splits[2], (TILES * TX, TY), 0, 8) < 7).astype(jnp.int32), jax.random.fold_in(splits[2], 1), 0, 1)
    volume = draw_volume(jax.random.fold_in(splits[5], 71), 0)
    face_runs = draw_face_runs(jax.random.fold_in(splits[5], 71), 0)
    return dict(omega=omega, conductance=conductance, wet=wet, volume=volume, face_runs=face_runs)


def diffuse(field, statics):
    cond_x = statics[0]
    cond_y = statics[1]
    cond_z = statics[2]
    wet_cells = statics[3]
    flux_x = cond_x[:, 1:, :] * (field[:, :, 1:, :] - field[:, :, :-1, :])
    flux_y = cond_y[:, :, 1:] * (field[:, :, :, 1:] - field[:, :, :, :-1])
    flux_z = cond_z[1:] * (field[:, 1:] - field[:, :-1])
    zero_level = jnp.zeros_like(field[:, :1])
    flux_z = jnp.concatenate([zero_level, flux_z, zero_level], axis=1)
    change = flux_x[:, :, 1:, 1:-1] - flux_x[:, :, :-1, 1:-1]
    change = change + flux_y[:, :, 1:-1, 1:] - flux_y[:, :, 1:-1, :-1]
    change = change + (flux_z[:, 1:] - flux_z[:, :-1])[:, :, 1:-1, 1:-1]
    return wet_cells[:, 1:-1, 1:-1] * (field[:, :, 1:-1, 1:-1] + change)

def to_grid(array):
    leading = array.shape[:-2]
    shaped = array.reshape(leading + (TGX, TGY, TX, TY))
    shaped = jnp.moveaxis(shaped, -2, -3)
    return shaped.reshape(leading + (TGX * TX, TGY * TY))

def to_tiles(array):
    leading = array.shape[:-2]
    shaped = array.reshape(leading + (TGX, TX, TGY, TY))
    shaped = jnp.moveaxis(shaped, -3, -2)
    return shaped.reshape(leading + (TGX * TGY * TX, TY))

def reference(omega, conductance, wet, volume, face_runs):
    row_ids = jnp.arange(TILES * TX, dtype=jnp.int32)
    rows_in = row_ids % TX
    runs = jnp.repeat(face_runs, TX, axis=0)
    col_ids = jnp.arange(TY, dtype=jnp.int32)
    open_x = (col_ids[None, :] >= runs[:, 0:1]) & (col_ids[None, :] < runs[:, 0:1] + runs[:, 1:2])
    factor_x = jnp.where(rows_in[:, None] == 0, open_x.astype(jnp.float32), jnp.float32(1.0))
    open_y = (rows_in >= runs[:, 2]) & (rows_in < runs[:, 2] + runs[:, 3])
    factor_y = jnp.where(col_ids[None, :] == 0, open_y[:, None].astype(jnp.float32), jnp.float32(1.0))
    level_ids = jnp.arange(LEV, dtype=jnp.int32)
    cond_z = conductance[2] * (level_ids > 0).astype(jnp.float32)[:, None, None]
    wet_float = wet.astype(jnp.float32)
    statics = jnp.stack([conductance[0] * factor_x[None], conductance[1] * factor_y[None], cond_z, jnp.broadcast_to(wet_float[None], (LEV, TILES * TX, TY))])
    statics_grid = jnp.pad(to_grid(statics), ((0, 0), (0, 0), (1, 1), (1, 1)))
    start = wet_float[None, None] * omega

    def run_block(block):
        field = to_grid(block)
        for sweep_index in range(ITERS):
            padded = jnp.pad(field, ((0, 0), (0, 0), (1, 1), (1, 1)))
            field = diffuse(padded, statics_grid)
        return to_tiles(field)
    blocks = start.reshape(VECS // 16, 16, LEV, TILES * TX, TY)
    diffused = lax.map(run_block, blocks).reshape(VECS, LEV, TILES * TX, TY)
    total_cells = LEV * TILES * TX * TY
    flat_values = diffused.reshape(VECS, -1)
    weighted = (diffused * volume[None, None]).reshape(VECS, -1)
    gram = lax.dot_general(weighted.astype(jnp.float32), flat_values.astype(jnp.float32), (((1,), (1,)), ((), ())), precision=lax.Precision.HIGHEST, preferred_element_type=jnp.float32) / total_cells
    r_factor = jnp.linalg.cholesky(gram).T
    return (diffused, r_factor)
```

```python
import functools
import jax
import jax.numpy as jnp
from jax import lax
from jax.sharding import PartitionSpec as P
from jax.experimental import pallas as pl
from jax.experimental.pallas import tpu as pltpu

MESH = pl.DeviceIdType.MESH
F32 = jnp.float32
LEV = 4
NG = 8
NCOEF = 7
CELLS = 4 * 512 * 128
HIGH = lax.Precision.HIGHEST


def did(t, v):
    return {"tiles": t, "vec": v}


def nt_dot(a, b):
    return lax.dot_general(a, b, (((1,), (1,)), ((), ())), precision=HIGH, preferred_element_type=F32)


def kernel(
    om, cond, wet, vol, runs,
    out, gram,
    om_v, halo, cond_v, wet_v, vol_v, runs_s,
    xm, xl, xr, cf, cbm, cbe,
    up_own, u_l, u_r, u_lr, u_h,
    buf_a, buf_b, fin, part, out_v,
    red_c, red_x, red_y, red_z,
    lsem, osem, hs, hr, ss, sr, es, er, us, ur, fs, fr, vs, vr, cs, cr, xs, xrs, ys, yr, zs, zr,
):
    t = lax.axis_index("tiles")
    v = lax.axis_index("vec")
    w = 1 - v
    core = lax.rem(t, 2)
    px = lax.rem(t // 2, 4)
    zh = lax.rem(t // 8, 2)
    py = t // 16
    tcol = lax.rem(t, 8)
    base = t - tcol
    up = lax.rem(t + 56, 64)
    down = lax.rem(t + 8, 64)
    left = base + lax.rem(tcol + 7, 8)
    right = base + lax.rem(tcol + 1, 8)
    pair = t + 1 - 2 * core
    zpair = t + 8 - 16 * zh
    x_peers = [t - 2 * px + 2 * lax.rem(px + d, 4) for d in (1, 2, 3)]
    y_peers = [t - 16 * py + 16 * lax.rem(py + d, 4) for d in (1, 2, 3)]

    loads = [
        pltpu.make_async_copy(cond, cond_v, lsem.at[0]),
        pltpu.make_async_copy(wet, wet_v, lsem.at[1]),
        pltpu.make_async_copy(runs, runs_s, lsem.at[2]),
        pltpu.make_async_copy(vol, vol_v, lsem.at[3]),
        pltpu.make_async_copy(om, om_v, lsem.at[4]),
    ]
    for cp in loads:
        cp.start()

    barrier = pltpu.get_barrier_semaphore()
    greet = [(up, v), (down, v), (left, v), (right, v)]
    greet += [(p, v) for p in x_peers] + [(p, v) for p in y_peers]
    greet += [(t, w), (zpair, w)]
    for p in greet:
        pl.semaphore_signal(barrier, inc=1, device_id=did(*p), device_id_type=MESH)

    for cp in loads[:3]:
        cp.wait()
    rows = lax.broadcasted_iota(jnp.int32, (8, 128), 0)
    cols = lax.broadcasted_iota(jnp.int32, (8, 128), 1)
    r0, r1, r2, r3 = (runs_s[0, k] for k in range(4))
    closed_x = (rows == 0) & ((cols < r0) | (cols >= r0 + r1))
    closed_y = (cols == 0) & ((rows < r2) | (rows >= r2 + r3))
    own = pl.ds(4, 8)
    for l in range(LEV):
        xm[l, own, :] = jnp.where(closed_x, 0.0, cond_v[0, l])
        xm[4 + l, own, :] = jnp.where(closed_y, 0.0, cond_v[1, l])
        xm[8 + l, own, :] = cond_v[2, l] if l else jnp.zeros((8, 128), F32)
    xm[12, own, :] = wet_v[...].astype(F32)

    pl.semaphore_wait(barrier, len(greet))

    def remote(src, dst, s, r, to):
        return pltpu.make_async_remote_copy(
            src_ref=src, dst_ref=dst, send_sem=s, recv_sem=r, device_id=did(*to), device_id_type=MESH
        )

    stat = [
        remote(xm.at[:, pl.ds(4, 4), :], xm.at[:, pl.ds(12, 4), :], ss.at[0], sr.at[0], (up, v)),
        remote(xm.at[:, pl.ds(8, 4), :], xm.at[:, pl.ds(0, 4), :], ss.at[1], sr.at[1], (down, v)),
    ]
    for cp in stat:
        cp.start()

    def halo_copy(g, d):
        blk = pl.ds(g * 32, 32)
        half = pl.ds(4 * d, 4)
        return remote(
            om.at[blk, half, :], halo.at[blk, half, :], hs.at[g, d], hr.at[g, d], (down if d else up, v)
        )

    for g in range(NG):
        for d in range(2):
            halo_copy(g, d).start()

    for cp in loads[3:]:
        cp.wait()
    om2 = om_v.reshape(2048, 128)
    halo2 = halo.reshape(2048, 128)
    out2 = out_v.reshape(2048, 128)

    def pack(g, c):
        for h in range(2):
            acc = jnp.zeros((8, 128), F32)
            for k in range(16):
                row = (k // 4) * 8 + 4 * h + k % 4
                val = om2[pl.ds(g * 256 + row, 8, stride=32), :]
                acc = jnp.where(cols // 8 == k, pltpu.roll(val, (k * 8 + 4) % 128, 1), acc)
            up_own[h, g] = acc
        return c

    lax.fori_loop(0, NG, pack, 0)
    edges = [
        remote(up_own, u_r, es.at[0], er.at[0], (left, v)),
        remote(up_own, u_l, es.at[1], er.at[1], (right, v)),
    ]
    for cp in edges:
        cp.start()

    for cp in stat:
        cp.wait_recv()
    stat_e = [
        remote(xm, xr, ss.at[2], sr.at[2], (left, v)),
        remote(xm, xl, ss.at[3], sr.at[3], (right, v)),
    ]
    for cp in stat_e:
        cp.start()

    for cp in edges:
        cp.wait_recv()

    def merge(g, c):
        for h in range(2):
            u_lr[h, g] = jnp.where(cols % 8 < 4, u_l[h, g], u_r[h, g])
        return c

    lax.fori_loop(0, NG, merge, 0)
    fwd = [
        remote(u_lr.at[0], u_h.at[0], us.at[0], ur.at[0], (up, v)),
        remote(u_lr.at[1], u_h.at[1], us.at[1], ur.at[1], (down, v)),
    ]
    for cp in fwd:
        cp.start()

    for cp in stat_e:
        cp.wait_recv()

    lanes = lax.broadcasted_iota(jnp.int32, (16, 128), 1)

    def both(k):
        return xm[k], jnp.where(lanes < 64, xr[k], xl[k])

    wets = both(12)
    for l in range(LEV):
        cxs, cys, czs = both(l), both(4 + l), both(8 + l)
        cps = both(9 + l) if l < 3 else (jnp.zeros((16, 128), F32),) * 2
        for e in range(2):
            cx, cy, cz, cp, wt = cxs[e], cys[e], czs[e], cps[e], wets[e]
            cxn = pltpu.roll(cx, 15, 0)
            cyn = pltpu.roll(jnp.where(lanes == 0, cys[1 - e], cy), 127, 1)
            total = cx + cxn + cy + cyn + cz + cp
            for k, val in enumerate((1.0 - total, cx, cxn, cy, cyn, cz, cp)):
                cf[e, l * NCOEF + k] = wt * val
    for e in range(2):
        cf[e, LEV * NCOEF] = wets[e]

    def spread(r, c):
        for e, dst in ((0, cbm), (1, cbe)):
            for k in range(LEV * NCOEF + 1):
                dst[r, k] = jnp.broadcast_to(cf[e, k, pl.ds(r, 1), :], (8, 128))
        return c

    lax.fori_loop(0, 16, spread, 0)
    for cp in fwd:
        cp.wait_recv()

    last = cols == 127
    first = cols == 0

    def vec_copy(g):
        grp = pl.ds(pl.multiple_of(g * 8, 8), 8)
        return remote(fin.at[pl.ds(w * 16, 16), grp, :], part.at[:, grp, :], vs.at[g], vr.at[g], (t, w))

    def out_copy(g):
        blk = pl.ds(g * 32, 32)
        return pltpu.make_async_copy(out_v.at[blk], out.at[blk], osem.at[g])

    def group(g, c):
        for d in range(2):
            halo_copy(g, d).wait_recv()
        for r in range(16):
            own_row = 4 <= r < 12
            hr_ = (r - 4) if own_row else (r + 4 if r < 4 else r - 12)
            src = om2 if own_row else halo2
            upk = u_lr if own_row else u_h
            wm = cbm[r, LEV * NCOEF]
            we = cbe[r, LEV * NCOEF]
            pk = upk[hr_ // 4, g]
            for l in range(LEV):
                k = l * 4 + hr_ % 4
                buf_a[r, 2 * l] = wm * src[pl.ds(g * 256 + l * 8 + hr_, 8, stride=32), :]
                buf_a[r, 2 * l + 1] = we * pltpu.roll(pk, (256 - (k * 8 + 4)) % 128, 1)
        bufs = (buf_a, buf_b)
        for p in range(4):
            src, dst = bufs[p % 2], bufs[(p + 1) % 2]

            def one_row(r, c, src=src, dst=dst, final=(p == 3)):
                mid = [[src[r, 2 * l + e] for e in range(2)] for l in range(LEV)]
                for l in range(LEV):
                    for e in range(1 if final else 2):
                        cb = cbe if e else cbm
                        me, other = mid[l][e], mid[l][1 - e]
                        f_l = pltpu.roll(jnp.where(last, other, me), 1, 1)
                        f_r = pltpu.roll(jnp.where(first, other, me), 127, 1)
                        k = l * NCOEF
                        acc = cb[r, k] * me
                        acc += cb[r, k + 1] * src[r - 1, 2 * l + e]
                        acc += cb[r, k + 2] * src[r + 1, 2 * l + e]
                        acc += cb[r, k + 3] * f_l
                        acc += cb[r, k + 4] * f_r
                        if l > 0:
                            acc += cb[r, k + 5] * mid[l - 1][e]
                        if l < 3:
                            acc += cb[r, k + 6] * mid[l + 1][e]
                        if final:
                            fin[l * 8 + r - 4, pl.ds(pl.multiple_of(g * 8, 8), 8), :] = acc
                            out2[pl.ds(g * 256 + l * 8 + r - 4, 8, stride=32), :] = acc
                        else:
                            dst[r, 2 * l + e] = acc
                return c

            lax.fori_loop(1 + p, 15 - p, one_row, 0)
        vec_copy(g).start()
        out_copy(g).start()
        return c

    lax.fori_loop(0, NG, group, 0)

    def own_block(i, acc):
        a = fin[i]
        return acc + nt_dot(a * vol_v[pl.ds(lax.rem(i, 8), 1), :], a)

    g_own = lax.fori_loop(0, 32, own_block, jnp.zeros((64, 64), F32))
    for g in range(NG):
        vec_copy(g).wait_recv()

    def cross_block(i, acc):
        mine, theirs = fin[v * 16 + i], part[i]
        a = jnp.where(v == 0, mine, theirs)
        b = jnp.where(v == 0, theirs, mine)
        return acc + nt_dot(a * vol_v[pl.ds(lax.rem(i, 8), 1), :], b)

    g_cross = lax.fori_loop(0, 16, cross_block, jnp.zeros((64, 64), F32))

    def stage(val, red, slot, peers, s, r):
        red[slot] = val
        cps = [remote(red.at[slot], red.at[slot], s.at[j], r.at[j], p) for j, p in enumerate(peers)]
        for cp in cps:
            cp.start()
        for cp in cps:
            cp.wait_recv()
        return cps

    sent = []
    val = jnp.concatenate([g_own, g_cross], axis=1)
    sent += stage(val, red_c, core, [(pair, v)], cs, cr)
    val = red_c[0] + red_c[1]
    sent += stage(val, red_x, px, [(p, v) for p in x_peers], xs, xrs)
    val = (red_x[0] + red_x[1]) + (red_x[2] + red_x[3])
    sent += stage(val, red_y, py, [(p, v) for p in y_peers], ys, yr)
    val = (red_y[0] + red_y[1]) + (red_y[2] + red_y[3])
    sent += stage(val, red_z, 2 * zh + v, [(t, w), (zpair, v), (zpair, w)], zs, zr)
    scale = 1.0 / CELLS
    even = red_z[0] + red_z[2]
    odd = red_z[1] + red_z[3]
    g00 = even[:, :64] * scale
    g11 = odd[:, :64] * scale
    g01 = (even[:, 64:] + odd[:, 64:]) * scale
    gram[pl.ds(0, 64), :] = jnp.concatenate([g00, g01], axis=1)
    gram[pl.ds(64, 64), :] = jnp.concatenate([g01.T, g11], axis=1)

    for cp in sent + stat + stat_e + edges + fwd:
        cp.wait_send()
    for g in range(NG):
        for d in range(2):
            halo_copy(g, d).wait_send()
        vec_copy(g).wait_send()
        out_copy(g).wait()


def shards(omega, conductance, wet, volume, face_runs):
    vm = lambda *s: pltpu.VMEM(s, F32)
    dma = lambda *s: pltpu.SemaphoreType.DMA(s)
    scratch = [
        vm(256, 8, 128), vm(256, 8, 128), vm(3, 4, 8, 128), pltpu.VMEM((8, 128), jnp.int32), vm(8, 128),
        pltpu.SMEM((1, 4), jnp.int32),
        vm(13, 16, 128), vm(13, 16, 128), vm(13, 16, 128), vm(2, 29, 16, 128),
        vm(16, 29, 8, 128), vm(16, 29, 8, 128),
        vm(2, 8, 8, 128), vm(2, 8, 8, 128), vm(2, 8, 8, 128), vm(2, 8, 8, 128), vm(2, 8, 8, 128),
        vm(16, 8, 8, 128), vm(16, 8, 8, 128), vm(32, 64, 128), vm(16, 64, 128), vm(256, 8, 128),
        vm(2, 64, 128), vm(4, 64, 128), vm(4, 64, 128), vm(4, 64, 128),
        dma(5), dma(8), dma(8, 2), dma(8, 2), dma(4), dma(4), dma(2), dma(2), dma(2), dma(2),
        dma(2), dma(2), dma(8), dma(8), dma(1), dma(1), dma(3), dma(3), dma(3), dma(3), dma(3), dma(3),
    ]
    anys = pl.BlockSpec(memory_space=pl.ANY)
    diffused, gram = pl.pallas_call(
        kernel,
        out_shape=(jax.ShapeDtypeStruct((256, 8, 128), F32), jax.ShapeDtypeStruct((128, 128), F32)),
        in_specs=[anys] * 5,
        out_specs=(anys, pl.BlockSpec(memory_space=pltpu.VMEM)),
        scratch_shapes=scratch,
        compiler_params=pltpu.CompilerParams(
            collective_id=0, has_side_effects=True, vmem_limit_bytes=48 * 1024 * 1024
        ),
        name="range_finder",
    )(omega.reshape(256, 8, 128), conductance, wet, volume, face_runs)
    r_factor = lax.linalg.cholesky(gram, symmetrize_input=False).T
    return (diffused.reshape(omega.shape), r_factor)


def solution(mesh):
    in_specs = (
        P("vec", None, "tiles", None),
        P(None, None, "tiles", None),
        P("tiles", None),
        P("tiles", None),
        P("tiles", None),
    )
    out_specs = (P("vec", None, "tiles", None), P())
    return jax.shard_map(shards, mesh=mesh, in_specs=in_specs, out_specs=out_specs, check_vma=False)
```

```python
import functools
import jax
import jax.numpy as jnp
from jax import lax
from jax.sharding import PartitionSpec as P
from jax.experimental import pallas as pl
from jax.experimental.pallas import tpu as pltpu

MESH = pl.DeviceIdType.MESH
F32 = jnp.float32
LEV = 4
NG = 8
NCOEF = 7
UNROLLS = (7, 6, 5)
EARLY = 2
KW = LEV * NCOEF
PAD = 40
CELLS = 4 * 512 * 128
HIGH = lax.Precision.HIGHEST


def did(t, v):
    return {"tiles": t, "vec": v}


def nt_dot(a, b):
    return lax.dot_general(a, b, (((1,), (1,)), ((), ())), precision=HIGH, preferred_element_type=F32)


def kernel(
    om, cond, wet, vol, runs,
    out, gram,
    om_v, halo, cond_v, wet_v, vol_v, runs_s,
    xm, xl, xr, cf, cbm, cbe,
    up_own, u_l, u_r, u_lr, u_h,
    buf, fin, part, out_v,
    red_c, red_x, red_y, red_z,
    lsem, osem, hs, hr, ss, sr, es, er, us, ur, fs, fr, vs, vr, cs, cr, xs, xrs, ys, yr, zs, zr,
):
    t = lax.axis_index("tiles")
    v = lax.axis_index("vec")
    w = 1 - v
    core = lax.rem(t, 2)
    px = lax.rem(t // 2, 4)
    zh = lax.rem(t // 8, 2)
    py = t // 16
    tcol = lax.rem(t, 8)
    base = t - tcol
    up = lax.rem(t + 56, 64)
    down = lax.rem(t + 8, 64)
    left = base + lax.rem(tcol + 7, 8)
    right = base + lax.rem(tcol + 1, 8)
    pair = t + 1 - 2 * core
    zpair = t + 8 - 16 * zh
    x_peers = [t - 2 * px + 2 * lax.rem(px + d, 4) for d in (1, 2, 3)]
    y_peers = [t - 16 * py + 16 * lax.rem(py + d, 4) for d in (1, 2, 3)]

    loads = [
        pltpu.make_async_copy(cond, cond_v, lsem.at[0]),
        pltpu.make_async_copy(wet, wet_v, lsem.at[1]),
        pltpu.make_async_copy(runs, runs_s, lsem.at[2]),
        pltpu.make_async_copy(vol, vol_v, lsem.at[3]),
        pltpu.make_async_copy(om, om_v.at[:, pl.ds(0, LEV)], lsem.at[4]),
    ]
    for cp in loads:
        cp.start()

    barrier = pltpu.get_barrier_semaphore()
    greet = [(up, v), (down, v), (left, v), (right, v)]
    greet += [(p, v) for p in x_peers] + [(p, v) for p in y_peers]
    greet += [(t, w), (zpair, w)]
    for p in greet:
        pl.semaphore_signal(barrier, inc=1, device_id=did(*p), device_id_type=MESH)

    for cp in loads[:3]:
        cp.wait()
    rows = lax.broadcasted_iota(jnp.int32, (8, 128), 0)
    cols = lax.broadcasted_iota(jnp.int32, (8, 128), 1)
    r0, r1, r2, r3 = (runs_s[0, k] for k in range(4))
    closed_x = (rows == 0) & ((cols < r0) | (cols >= r0 + r1))
    closed_y = (cols == 0) & ((rows < r2) | (rows >= r2 + r3))
    own = pl.ds(4, 8)
    for l in range(LEV):
        xm[l, own, :] = jnp.where(closed_x, 0.0, cond_v[0, l])
        xm[4 + l, own, :] = jnp.where(closed_y, 0.0, cond_v[1, l])
        xm[8 + l, own, :] = cond_v[2, l] if l else jnp.zeros((8, 128), F32)
    xm[12, own, :] = wet_v[...].astype(F32)

    pl.semaphore_wait(barrier, len(greet))

    def remote(src, dst, s, r, to):
        return pltpu.make_async_remote_copy(
            src_ref=src, dst_ref=dst, send_sem=s, recv_sem=r, device_id=did(*to), device_id_type=MESH
        )

    stat = [
        remote(xm.at[:, pl.ds(4, 4), :], xm.at[:, pl.ds(12, 4), :], ss.at[0], sr.at[0], (up, v)),
        remote(xm.at[:, pl.ds(8, 4), :], xm.at[:, pl.ds(0, 4), :], ss.at[1], sr.at[1], (down, v)),
    ]
    for cp in stat:
        cp.start()

    def halo_copy(g, d):
        blk = pl.ds(g * 8, 8)
        half = pl.ds(4 * d, 4)
        return remote(
            om.at[blk, :, half, :], halo.at[blk, pl.ds(0, LEV), half, :], hs.at[g, d], hr.at[g, d], (down if d else up, v)
        )

    def send_halos(g, c):
        for d in range(2):
            halo_copy(g, d).start()
        return c

    lax.fori_loop(0, EARLY, send_halos, 0)

    for cp in loads[3:]:
        cp.wait()
    om2 = om_v.reshape(64 * PAD, 128)
    halo2 = halo.reshape(64 * PAD, 128)
    out2 = out_v.reshape(64 * PAD, 128)

    def pack(g, c):
        for h in range(2):
            acc = jnp.zeros((8, 128), F32)
            for k in range(16):
                row = (k // 4) * 8 + 4 * h + k % 4
                val = om2[pl.ds(g * 8 * PAD + row, 8, stride=PAD), :]
                acc = jnp.where(cols // 8 == k, pltpu.roll(val, (k * 8 + 4) % 128, 1), acc)
            up_own[h, g] = acc
        return c

    lax.fori_loop(0, NG, pack, 0)
    edges = [
        remote(up_own, u_r, es.at[0], er.at[0], (left, v)),
        remote(up_own, u_l, es.at[1], er.at[1], (right, v)),
    ]
    for cp in edges:
        cp.start()

    for cp in stat:
        cp.wait_recv()
    stat_e = [
        remote(xm, xr, ss.at[2], sr.at[2], (left, v)),
        remote(xm, xl, ss.at[3], sr.at[3], (right, v)),
    ]
    for cp in stat_e:
        cp.start()

    for cp in edges:
        cp.wait_recv()

    def merge(g, c):
        for h in range(2):
            u_lr[h, g] = jnp.where(cols % 8 < 4, u_l[h, g], u_r[h, g])
        return c

    lax.fori_loop(0, NG, merge, 0)
    fwd = [
        remote(u_lr.at[0], u_h.at[0], us.at[0], ur.at[0], (up, v)),
        remote(u_lr.at[1], u_h.at[1], us.at[1], ur.at[1], (down, v)),
    ]
    for cp in fwd:
        cp.start()
    lax.fori_loop(EARLY, NG, send_halos, 0)

    for cp in stat_e:
        cp.wait_recv()

    lanes = lax.broadcasted_iota(jnp.int32, (16, 128), 1)

    def both(k):
        return xm[k], jnp.where(lanes < 64, xr[k], xl[k])

    wets = both(12)
    for l in range(LEV):
        cxs, cys, czs = both(l), both(4 + l), both(8 + l)
        cps = both(9 + l) if l < 3 else (jnp.zeros((16, 128), F32),) * 2
        for e in range(2):
            cx, cy, cz, cp, wt = cxs[e], cys[e], czs[e], cps[e], wets[e]
            cxn = pltpu.roll(cx, 15, 0)
            cyn = pltpu.roll(jnp.where(lanes == 0, cys[1 - e], cy), 127, 1)
            total = cx + cxn + cy + cyn + cz + cp
            for k, val in enumerate((1.0 - total, cx, cxn, cy, cyn, cz, cp)):
                cf[e, l * NCOEF + k] = wt * val
    for e in range(2):
        cf[e, LEV * NCOEF] = wets[e]

    def spread(r, c):
        for e, dst in ((0, cbm), (1, cbe)):
            for k in range(LEV * NCOEF + 1):
                dst[r, k] = jnp.broadcast_to(cf[e, k, pl.ds(r, 1), :], (8, 128))
        return c

    lax.fori_loop(0, 16, spread, 0)
    for cp in fwd:
        cp.wait_recv()

    last = cols == 127
    first = cols == 0

    def vec_copy(g):
        grp = pl.ds(pl.multiple_of(g * 8, 8), 8)
        return remote(fin.at[pl.ds(w * 16, 16), grp, :], part.at[:, grp, :], vs.at[g], vr.at[g], (t, w))

    def out_copy(g):
        blk = pl.ds(g * 8, 8)
        return pltpu.make_async_copy(out_v.at[blk, pl.ds(0, LEV)], out.at[blk], osem.at[g])

    def group(g, c):
        for d in range(2):
            halo_copy(g, d).wait_recv()
        def load_row(i, c):
            at = g * 8 * PAD + i
            for src, upk, r in ((om2, u_lr, i + 4), (halo2, u_h, lax.rem(i + 12, 16))):
                pk = upk[i // 4, g]
                for l in range(LEV):
                    k = l * 4 + lax.rem(i, 4)
                    buf[0, r, 2 * l] = cbm[r, KW] * src[pl.ds(at + l * 8, 8, stride=PAD), :]
                    buf[0, r, 2 * l + 1] = cbe[r, KW] * pltpu.roll(pk, lax.rem(252 - k * 8, 128), 1)
            return c

        lax.fori_loop(0, 8, load_row, 0)

        def rows_at(src, dst, rs, final):
            for r in rs:
                mid = [[buf[src, r, 2 * l + e] for e in range(2)] for l in range(LEV)]
                for l in range(LEV):
                    for e in range(1 if final else 2):
                        cb = cbe if e else cbm
                        me, other = mid[l][e], mid[l][1 - e]
                        f_l = pltpu.roll(jnp.where(last, other, me), 1, 1)
                        f_r = pltpu.roll(jnp.where(first, other, me), 127, 1)
                        k = l * NCOEF
                        acc = cb[r, k] * me
                        acc += cb[r, k + 1] * buf[src, r - 1, 2 * l + e] + cb[r, k + 2] * buf[src, r + 1, 2 * l + e]
                        if l > 0:
                            acc += cb[r, k + 5] * mid[l - 1][e]
                        if l < 3:
                            acc += cb[r, k + 6] * mid[l + 1][e]
                        acc += cb[r, k + 3] * f_l + cb[r, k + 4] * f_r
                        if final:
                            fin[l * 8 + r - 4, pl.ds(pl.multiple_of(g * 8, 8), 8), :] = acc
                            out2[pl.ds(g * 8 * PAD + l * 8 + r - 4, 8, stride=PAD), :] = acc
                        else:
                            buf[dst, r, 2 * l + e] = acc

        for p in range(3):
            size = UNROLLS[p]

            def step(i, c, p=p, size=size):
                rows_at(p % 2, 1 - p % 2, [1 + p + size * i + j for j in range(size)], False)
                return c

            lax.fori_loop(0, (14 - 2 * p) // size, step, 0)

        def last_pass(i, c):
            rows_at(1, 0, [4 + 4 * i + j for j in range(4)], True)
            return c

        lax.fori_loop(0, 2, last_pass, 0)
        vec_copy(g).start()
        out_copy(g).start()
        return c

    lax.fori_loop(0, NG, group, 0)

    def own_block(i, acc):
        a = fin[i]
        return acc + nt_dot(a * vol_v[pl.ds(lax.rem(i, 8), 1), :], a)

    g_own = lax.fori_loop(0, 32, own_block, jnp.zeros((64, 64), F32))
    for g in range(NG):
        vec_copy(g).wait_recv()

    def cross_block(i, acc):
        mine, theirs = fin[v * 16 + i], part[i]
        a = jnp.where(v == 0, mine, theirs)
        b = jnp.where(v == 0, theirs, mine)
        return acc + nt_dot(a * vol_v[pl.ds(lax.rem(i, 8), 1), :], b)

    g_cross = lax.fori_loop(0, 16, cross_block, jnp.zeros((64, 64), F32))

    def stage(val, red, slot, peers, s, r):
        red[slot] = val
        cps = [remote(red.at[slot], red.at[slot], s.at[j], r.at[j], p) for j, p in enumerate(peers)]
        for cp in cps:
            cp.start()
        for cp in cps:
            cp.wait_recv()
        return cps

    sent = []
    val = jnp.concatenate([g_own, g_cross], axis=1)
    sent += stage(val, red_c, core, [(pair, v)], cs, cr)
    val = red_c[0] + red_c[1]
    sent += stage(val, red_x, px, [(p, v) for p in x_peers], xs, xrs)
    val = (red_x[0] + red_x[1]) + (red_x[2] + red_x[3])
    sent += stage(val, red_y, py, [(p, v) for p in y_peers], ys, yr)
    val = (red_y[0] + red_y[1]) + (red_y[2] + red_y[3])
    sent += stage(val, red_z, 2 * zh + v, [(t, w), (zpair, v), (zpair, w)], zs, zr)
    scale = 1.0 / CELLS
    even = red_z[0] + red_z[2]
    odd = red_z[1] + red_z[3]
    g00 = even[:, :64] * scale
    g11 = odd[:, :64] * scale
    g01 = (even[:, 64:] + odd[:, 64:]) * scale
    gram[pl.ds(0, 64), :] = jnp.concatenate([g00, g01], axis=1)
    gram[pl.ds(64, 64), :] = jnp.concatenate([g01.T, g11], axis=1)

    for cp in sent + stat + stat_e + edges + fwd:
        cp.wait_send()
    for g in range(NG):
        for d in range(2):
            halo_copy(g, d).wait_send()
        vec_copy(g).wait_send()
        out_copy(g).wait()


def shards(omega, conductance, wet, volume, face_runs):
    vm = lambda *s: pltpu.VMEM(s, F32)
    dma = lambda *s: pltpu.SemaphoreType.DMA(s)
    scratch = [
        vm(64, 5, 8, 128), vm(64, 5, 8, 128), vm(3, 4, 8, 128), pltpu.VMEM((8, 128), jnp.int32), vm(8, 128),
        pltpu.SMEM((1, 4), jnp.int32),
        vm(13, 16, 128), vm(13, 16, 128), vm(13, 16, 128), vm(2, 29, 16, 128),
        vm(16, 29, 8, 128), vm(16, 29, 8, 128),
        vm(2, 8, 8, 128), vm(2, 8, 8, 128), vm(2, 8, 8, 128), vm(2, 8, 8, 128), vm(2, 8, 8, 128),
        vm(2, 16, 8, 8, 128), vm(32, 64, 128), vm(16, 64, 128), vm(64, 5, 8, 128),
        vm(2, 64, 128), vm(4, 64, 128), vm(4, 64, 128), vm(4, 64, 128),
        dma(5), dma(8), dma(8, 2), dma(8, 2), dma(4), dma(4), dma(2), dma(2), dma(2), dma(2),
        dma(2), dma(2), dma(8), dma(8), dma(1), dma(1), dma(3), dma(3), dma(3), dma(3), dma(3), dma(3),
    ]
    anys = pl.BlockSpec(memory_space=pl.ANY)
    diffused, gram = pl.pallas_call(
        kernel,
        out_shape=(jax.ShapeDtypeStruct((64, LEV, 8, 128), F32), jax.ShapeDtypeStruct((128, 128), F32)),
        in_specs=[anys] * 5,
        out_specs=(anys, pl.BlockSpec(memory_space=pltpu.VMEM)),
        scratch_shapes=scratch,
        compiler_params=pltpu.CompilerParams(
            collective_id=0, has_side_effects=True, vmem_limit_bytes=48 * 1024 * 1024
        ),
        name="range_finder",
    )(omega, conductance, wet, volume, face_runs)
    r_factor = lax.linalg.cholesky(gram, symmetrize_input=False).T
    return (diffused, r_factor)


def solution(mesh):
    in_specs = (
        P("vec", None, "tiles", None),
        P(None, None, "tiles", None),
        P("tiles", None),
        P("tiles", None),
        P("tiles", None),
    )
    out_specs = (P("vec", None, "tiles", None), P())
    return jax.shard_map(shards, mesh=mesh, in_specs=in_specs, out_specs=out_specs, check_vma=False)
```

```python
import functools
import jax
import jax.numpy as jnp
from jax import lax
from jax.sharding import PartitionSpec as P
from jax.experimental import pallas as pl
from jax.experimental.pallas import tpu as pltpu

MESH = pl.DeviceIdType.MESH
F32 = jnp.float32
LEV = 4
NG = 8
NCOEF = 7
UNROLLS = (7, 6, 5)
EARLY = 4
KW = LEV * NCOEF
GRAM_ROWS = 4
PAD = 40
CELLS = 4 * 512 * 128
HIGH = lax.Precision.HIGHEST


def did(t, v):
    return {"tiles": t, "vec": v}


def nt_dot(a, b):
    return lax.dot_general(a, b, (((1,), (1,)), ((), ())), precision=HIGH, preferred_element_type=F32)


def kernel(
    om, cond, wet, vol, runs,
    out, gram,
    om_v, halo, cond_v, wet_v, vol_v, runs_s,
    xm, xl, xr, cf, cbm, cbe,
    up_own, u_l, u_r, u_lr, u_h,
    buf, fin, part,
    red_c, red_x, red_y, red_z,
    lsem, hs, hr, ss, sr, es, er, us, ur, fs, fr, vs, vr, cs, cr, xs, xrs, ys, yr, zs, zr,
):
    t = lax.axis_index("tiles")
    v = lax.axis_index("vec")
    w = 1 - v
    core = lax.rem(t, 2)
    px = lax.rem(t // 2, 4)
    zh = lax.rem(t // 8, 2)
    py = t // 16
    tcol = lax.rem(t, 8)
    base = t - tcol
    up = lax.rem(t + 56, 64)
    down = lax.rem(t + 8, 64)
    left = base + lax.rem(tcol + 7, 8)
    right = base + lax.rem(tcol + 1, 8)
    pair = t + 1 - 2 * core
    zpair = t + 8 - 16 * zh
    x_peers = [t - 2 * px + 2 * lax.rem(px + d, 4) for d in (1, 2, 3)]
    y_peers = [t - 16 * py + 16 * lax.rem(py + d, 4) for d in (1, 2, 3)]

    loads = [
        pltpu.make_async_copy(cond, cond_v, lsem.at[0]),
        pltpu.make_async_copy(wet, wet_v, lsem.at[1]),
        pltpu.make_async_copy(runs, runs_s, lsem.at[2]),
        pltpu.make_async_copy(vol, vol_v, lsem.at[3]),
        pltpu.make_async_copy(om, om_v.at[:, pl.ds(0, LEV)], lsem.at[4]),
    ]
    for cp in loads:
        cp.start()

    barrier = pltpu.get_barrier_semaphore()
    greet = [(up, v), (down, v), (left, v), (right, v)]
    greet += [(p, v) for p in x_peers] + [(p, v) for p in y_peers]
    greet += [(t, w), (zpair, w)]
    for p in greet:
        pl.semaphore_signal(barrier, inc=1, device_id=did(*p), device_id_type=MESH)

    for cp in loads[:3]:
        cp.wait()
    rows = lax.broadcasted_iota(jnp.int32, (8, 128), 0)
    cols = lax.broadcasted_iota(jnp.int32, (8, 128), 1)
    r0, r1, r2, r3 = (runs_s[0, k] for k in range(4))
    closed_x = (rows == 0) & ((cols < r0) | (cols >= r0 + r1))
    closed_y = (cols == 0) & ((rows < r2) | (rows >= r2 + r3))
    own = pl.ds(4, 8)
    for l in range(LEV):
        xm[l, own, :] = jnp.where(closed_x, 0.0, cond_v[0, l])
        xm[4 + l, own, :] = jnp.where(closed_y, 0.0, cond_v[1, l])
        xm[8 + l, own, :] = cond_v[2, l] if l else jnp.zeros((8, 128), F32)
    xm[12, own, :] = wet_v[...].astype(F32)

    pl.semaphore_wait(barrier, len(greet))

    def remote(src, dst, s, r, to):
        return pltpu.make_async_remote_copy(
            src_ref=src, dst_ref=dst, send_sem=s, recv_sem=r, device_id=did(*to), device_id_type=MESH
        )

    stat = [
        remote(xm.at[:, pl.ds(4, 4), :], xm.at[:, pl.ds(12, 4), :], ss.at[0], sr.at[0], (up, v)),
        remote(xm.at[:, pl.ds(8, 4), :], xm.at[:, pl.ds(0, 4), :], ss.at[1], sr.at[1], (down, v)),
    ]
    for cp in stat:
        cp.start()

    def halo_copy(g, d):
        blk = pl.ds(g * 8, 8)
        half = pl.ds(4 * d, 4)
        return remote(
            om.at[blk, :, half, :], halo.at[blk, pl.ds(0, LEV), half, :], hs.at[g, d], hr.at[g, d], (down if d else up, v)
        )

    def send_halos(g, c):
        for d in range(2):
            halo_copy(g, d).start()
        return c

    lax.fori_loop(0, EARLY, send_halos, 0)

    for cp in loads[3:]:
        cp.wait()
    om2 = om_v.reshape(64 * PAD, 128)
    halo2 = halo.reshape(64 * PAD, 128)
    out2 = out.reshape(64 * 32, 128)

    def pack(g, c):
        for h in range(2):
            acc = jnp.zeros((8, 128), F32)
            for k in range(16):
                row = (k // 4) * 8 + 4 * h + k % 4
                val = om2[pl.ds(g * 8 * PAD + row, 8, stride=PAD), :]
                acc = jnp.where(cols // 8 == k, pltpu.roll(val, (k * 8 + 4) % 128, 1), acc)
            up_own[h, g] = acc
        return c

    lax.fori_loop(0, NG, pack, 0)
    edges = [
        remote(up_own, u_r, es.at[0], er.at[0], (left, v)),
        remote(up_own, u_l, es.at[1], er.at[1], (right, v)),
    ]
    for cp in edges:
        cp.start()

    for cp in stat:
        cp.wait_recv()
    stat_e = [
        remote(xm, xr, ss.at[2], sr.at[2], (left, v)),
        remote(xm, xl, ss.at[3], sr.at[3], (right, v)),
    ]
    for cp in stat_e:
        cp.start()

    for cp in edges:
        cp.wait_recv()

    def merge(g, c):
        for h in range(2):
            u_lr[h, g] = jnp.where(cols % 8 < 4, u_l[h, g], u_r[h, g])
        return c

    lax.fori_loop(0, NG, merge, 0)
    fwd = [
        remote(u_lr.at[0], u_h.at[0], us.at[0], ur.at[0], (up, v)),
        remote(u_lr.at[1], u_h.at[1], us.at[1], ur.at[1], (down, v)),
    ]
    for cp in fwd:
        cp.start()
    lax.fori_loop(EARLY, NG, send_halos, 0)

    for cp in stat_e:
        cp.wait_recv()

    lanes = lax.broadcasted_iota(jnp.int32, (16, 128), 1)

    def both(k):
        return xm[k], jnp.where(lanes < 64, xr[k], xl[k])

    wets = both(12)
    for l in range(LEV):
        cxs, cys, czs = both(l), both(4 + l), both(8 + l)
        cps = both(9 + l) if l < 3 else (jnp.zeros((16, 128), F32),) * 2
        for e in range(2):
            cx, cy, cz, cp, wt = cxs[e], cys[e], czs[e], cps[e], wets[e]
            cxn = pltpu.roll(cx, 15, 0)
            cyn = pltpu.roll(jnp.where(lanes == 0, cys[1 - e], cy), 127, 1)
            total = cx + cxn + cy + cyn + cz + cp
            for k, val in enumerate((1.0 - total, cx, cxn, cy, cyn, cz, cp)):
                cf[e, l * NCOEF + k] = wt * val
    for e in range(2):
        cf[e, LEV * NCOEF] = wets[e]

    def spread(r, c):
        for e, dst in ((0, cbm), (1, cbe)):
            for k in range(LEV * NCOEF + 1):
                dst[r, k] = jnp.broadcast_to(cf[e, k, pl.ds(r, 1), :], (8, 128))
        return c

    lax.fori_loop(0, 16, spread, 0)
    for cp in fwd:
        cp.wait_recv()

    last = cols == 127
    first = cols == 0

    def vec_copy(g):
        grp = pl.ds(pl.multiple_of(g * 8, 8), 8)
        return remote(fin.at[pl.ds(w * 16, 16), grp, :], part.at[:, grp, :], vs.at[g], vr.at[g], (t, w))

    def group(g, c):
        for d in range(2):
            halo_copy(g, d).wait_recv()
        def load_row(i, c):
            at = g * 8 * PAD + i
            for src, upk, r in ((om2, u_lr, i + 4), (halo2, u_h, lax.rem(i + 12, 16))):
                pk = upk[i // 4, g]
                for l in range(LEV):
                    k = l * 4 + lax.rem(i, 4)
                    buf[0, r, 2 * l] = cbm[r, KW] * src[pl.ds(at + l * 8, 8, stride=PAD), :]
                    buf[0, r, 2 * l + 1] = cbe[r, KW] * pltpu.roll(pk, lax.rem(252 - k * 8, 128), 1)
            return c

        lax.fori_loop(0, 8, load_row, 0)

        def rows_at(src, dst, rs, final):
            for r in rs:
                mid = [[buf[src, r, 2 * l + e] for e in range(2)] for l in range(LEV)]
                for l in range(LEV):
                    for e in range(1 if final else 2):
                        cb = cbe if e else cbm
                        me, other = mid[l][e], mid[l][1 - e]
                        f_l = pltpu.roll(jnp.where(last, other, me), 1, 1)
                        f_r = pltpu.roll(jnp.where(first, other, me), 127, 1)
                        k = l * NCOEF
                        acc = cb[r, k] * me
                        acc += cb[r, k + 1] * buf[src, r - 1, 2 * l + e] + cb[r, k + 2] * buf[src, r + 1, 2 * l + e]
                        if l > 0:
                            acc += cb[r, k + 5] * mid[l - 1][e]
                        if l < 3:
                            acc += cb[r, k + 6] * mid[l + 1][e]
                        acc += cb[r, k + 3] * f_l + cb[r, k + 4] * f_r
                        if final:
                            fin[l * 8 + r - 4, pl.ds(pl.multiple_of(g * 8, 8), 8), :] = acc
                            out2[pl.ds(g * 256 + l * 8 + r - 4, 8, stride=32), :] = acc
                        else:
                            buf[dst, r, 2 * l + e] = acc

        for p in range(3):
            size = UNROLLS[p]

            def step(i, c, p=p, size=size):
                rows_at(p % 2, 1 - p % 2, [1 + p + size * i + j for j in range(size)], False)
                return c

            lax.fori_loop(0, (14 - 2 * p) // size, step, 0)

        def last_pass(i, c):
            rows_at(1, 0, [4 + 4 * i + j for j in range(4)], True)
            return c

        lax.fori_loop(0, 2, last_pass, 0)
        vec_copy(g).start()
        return c

    lax.fori_loop(0, NG, group, 0)

    def wide(take, i):
        return jnp.concatenate([take(i * GRAM_ROWS + j) for j in range(GRAM_ROWS)], axis=1)

    def weights(i):
        return wide(lambda k: vol_v[pl.ds(lax.rem(k, 8), 1), :], i)

    def own_block(i, acc):
        a = wide(lambda k: fin[k], i)
        return acc + nt_dot(a * weights(i), a)

    g_own = lax.fori_loop(0, 32 // GRAM_ROWS, own_block, jnp.zeros((64, 64), F32))
    for g in range(NG):
        vec_copy(g).wait_recv()

    def cross_block(i, acc):
        mine, theirs = wide(lambda k: fin[v * 16 + k], i), wide(lambda k: part[k], i)
        a = jnp.where(v == 0, mine, theirs)
        b = jnp.where(v == 0, theirs, mine)
        return acc + nt_dot(a * weights(i), b)

    g_cross = lax.fori_loop(0, 16 // GRAM_ROWS, cross_block, jnp.zeros((64, 64), F32))

    def stage(val, red, slot, peers, s, r):
        red[slot] = val
        cps = [remote(red.at[slot], red.at[slot], s.at[j], r.at[j], p) for j, p in enumerate(peers)]
        for cp in cps:
            cp.start()
        for cp in cps:
            cp.wait_recv()
        return cps

    sent = []
    val = jnp.concatenate([g_own, g_cross], axis=1)
    sent += stage(val, red_c, core, [(pair, v)], cs, cr)
    val = red_c[0] + red_c[1]
    sent += stage(val, red_x, px, [(p, v) for p in x_peers], xs, xrs)
    val = (red_x[0] + red_x[1]) + (red_x[2] + red_x[3])
    sent += stage(val, red_y, py, [(p, v) for p in y_peers], ys, yr)
    val = (red_y[0] + red_y[1]) + (red_y[2] + red_y[3])
    sent += stage(val, red_z, 2 * zh + v, [(t, w), (zpair, v), (zpair, w)], zs, zr)
    scale = 1.0 / CELLS
    even = red_z[0] + red_z[2]
    odd = red_z[1] + red_z[3]
    g00 = even[:, :64] * scale
    g11 = odd[:, :64] * scale
    g01 = (even[:, 64:] + odd[:, 64:]) * scale
    gram[pl.ds(0, 64), :] = jnp.concatenate([g00, g01], axis=1)
    gram[pl.ds(64, 64), :] = jnp.concatenate([g01.T, g11], axis=1)

    for cp in sent + stat + stat_e + edges + fwd:
        cp.wait_send()
    for g in range(NG):
        for d in range(2):
            halo_copy(g, d).wait_send()
        vec_copy(g).wait_send()


def shards(omega, conductance, wet, volume, face_runs):
    vm = lambda *s: pltpu.VMEM(s, F32)
    dma = lambda *s: pltpu.SemaphoreType.DMA(s)
    scratch = [
        vm(64, 5, 8, 128), vm(64, 5, 8, 128), vm(3, 4, 8, 128), pltpu.VMEM((8, 128), jnp.int32), vm(8, 128),
        pltpu.SMEM((1, 4), jnp.int32),
        vm(13, 16, 128), vm(13, 16, 128), vm(13, 16, 128), vm(2, 29, 16, 128),
        vm(16, 29, 8, 128), vm(16, 29, 8, 128),
        vm(2, 8, 8, 128), vm(2, 8, 8, 128), vm(2, 8, 8, 128), vm(2, 8, 8, 128), vm(2, 8, 8, 128),
        vm(2, 16, 8, 8, 128), vm(32, 64, 128), vm(16, 64, 128),
        vm(2, 64, 128), vm(4, 64, 128), vm(4, 64, 128), vm(4, 64, 128),
        dma(5), dma(8, 2), dma(8, 2), dma(4), dma(4), dma(2), dma(2), dma(2), dma(2),
        dma(2), dma(2), dma(8), dma(8), dma(1), dma(1), dma(3), dma(3), dma(3), dma(3), dma(3), dma(3),
    ]
    anys = pl.BlockSpec(memory_space=pl.ANY)
    diffused, gram = pl.pallas_call(
        kernel,
        out_shape=(jax.ShapeDtypeStruct((64, LEV, 8, 128), F32), jax.ShapeDtypeStruct((128, 128), F32)),
        in_specs=[anys] * 5,
        out_specs=(pl.BlockSpec(memory_space=pltpu.VMEM),) * 2,
        scratch_shapes=scratch,
        compiler_params=pltpu.CompilerParams(
            collective_id=0, has_side_effects=True, vmem_limit_bytes=67043328
        ),
        name="range_finder",
    )(omega, conductance, wet, volume, face_runs)
    r_factor = lax.linalg.cholesky(gram, symmetrize_input=False).T
    return (diffused, r_factor)


def solution(mesh):
    in_specs = (
        P("vec", None, "tiles", None),
        P(None, None, "tiles", None),
        P("tiles", None),
        P("tiles", None),
        P("tiles", None),
    )
    out_specs = (P("vec", None, "tiles", None), P())
    return jax.shard_map(shards, mesh=mesh, in_specs=in_specs, out_specs=out_specs, check_vma=False)
```

```python
import functools
import jax
import jax.numpy as jnp
from jax import lax
from jax.sharding import PartitionSpec as P
from jax.experimental import pallas as pl
from jax.experimental.pallas import tpu as pltpu

MESH = pl.DeviceIdType.MESH
F32 = jnp.float32
LEV = 4
NG = 8
NCOEF = 7
UNROLLS = (7, 6, 5)
EARLY = 4
KW = LEV * NCOEF
GRAM_ROWS = 4
PANEL = 16
PAD = 40
CELLS = 4 * 512 * 128
HIGH = lax.Precision.HIGHEST


def did(t, v):
    return {"tiles": t, "vec": v}


def nt_dot(a, b):
    return lax.dot_general(a, b, (((1,), (1,)), ((), ())), precision=HIGH, preferred_element_type=F32)


def kernel(
    om, cond, wet, vol, runs,
    out, gram,
    om_v, halo, cond_v, wet_v, vol_v, runs_s,
    xm, xl, xr, cf, cbm, cbe,
    up_own, u_l, u_r, u_lr, u_h,
    buf, fin, part,
    red_c, red_x, red_y, red_z,
    lsem, hs, hr, ss, sr, es, er, us, ur, fs, fr, vs, vr, cs, cr, xs, xrs, ys, yr, zs, zr,
):
    t = lax.axis_index("tiles")
    v = lax.axis_index("vec")
    w = 1 - v
    core = lax.rem(t, 2)
    px = lax.rem(t // 2, 4)
    zh = lax.rem(t // 8, 2)
    py = t // 16
    tcol = lax.rem(t, 8)
    base = t - tcol
    up = lax.rem(t + 56, 64)
    down = lax.rem(t + 8, 64)
    left = base + lax.rem(tcol + 7, 8)
    right = base + lax.rem(tcol + 1, 8)
    pair = t + 1 - 2 * core
    zpair = t + 8 - 16 * zh
    x_peers = [t - 2 * px + 2 * lax.rem(px + d, 4) for d in (1, 2, 3)]
    y_peers = [t - 16 * py + 16 * lax.rem(py + d, 4) for d in (1, 2, 3)]

    loads = [
        pltpu.make_async_copy(cond, cond_v, lsem.at[0]),
        pltpu.make_async_copy(wet, wet_v, lsem.at[1]),
        pltpu.make_async_copy(runs, runs_s, lsem.at[2]),
        pltpu.make_async_copy(vol, vol_v, lsem.at[3]),
        pltpu.make_async_copy(om, om_v.at[:, pl.ds(0, LEV)], lsem.at[4]),
    ]
    for cp in loads:
        cp.start()

    barrier = pltpu.get_barrier_semaphore()
    greet = [(up, v), (down, v), (left, v), (right, v)]
    greet += [(p, v) for p in x_peers] + [(p, v) for p in y_peers]
    greet += [(t, w), (zpair, w)]
    for p in greet:
        pl.semaphore_signal(barrier, inc=1, device_id=did(*p), device_id_type=MESH)

    for cp in loads[:3]:
        cp.wait()
    rows = lax.broadcasted_iota(jnp.int32, (8, 128), 0)
    cols = lax.broadcasted_iota(jnp.int32, (8, 128), 1)
    r0, r1, r2, r3 = (runs_s[0, k] for k in range(4))
    closed_x = (rows == 0) & ((cols < r0) | (cols >= r0 + r1))
    closed_y = (cols == 0) & ((rows < r2) | (rows >= r2 + r3))
    own = pl.ds(4, 8)
    for l in range(LEV):
        xm[l, own, :] = jnp.where(closed_x, 0.0, cond_v[0, l])
        xm[4 + l, own, :] = jnp.where(closed_y, 0.0, cond_v[1, l])
        xm[8 + l, own, :] = cond_v[2, l] if l else jnp.zeros((8, 128), F32)
    xm[12, own, :] = wet_v[...].astype(F32)

    pl.semaphore_wait(barrier, len(greet))

    def remote(src, dst, s, r, to):
        return pltpu.make_async_remote_copy(
            src_ref=src, dst_ref=dst, send_sem=s, recv_sem=r, device_id=did(*to), device_id_type=MESH
        )

    stat = [
        remote(xm.at[:, pl.ds(4, 4), :], xm.at[:, pl.ds(12, 4), :], ss.at[0], sr.at[0], (up, v)),
        remote(xm.at[:, pl.ds(8, 4), :], xm.at[:, pl.ds(0, 4), :], ss.at[1], sr.at[1], (down, v)),
    ]
    for cp in stat:
        cp.start()

    def halo_copy(g, d):
        blk = pl.ds(g * 8, 8)
        half = pl.ds(4 * d, 4)
        return remote(
            om.at[blk, :, half, :], halo.at[blk, pl.ds(0, LEV), half, :], hs.at[g, d], hr.at[g, d], (down if d else up, v)
        )

    def send_halos(g, c):
        for d in range(2):
            halo_copy(g, d).start()
        return c

    lax.fori_loop(0, EARLY, send_halos, 0)

    for cp in loads[3:]:
        cp.wait()
    om2 = om_v.reshape(64 * PAD, 128)
    halo2 = halo.reshape(64 * PAD, 128)
    out2 = out.reshape(64 * 32, 128)

    def pack(g, c):
        for h in range(2):
            acc = jnp.zeros((8, 128), F32)
            for k in range(16):
                row = (k // 4) * 8 + 4 * h + k % 4
                val = om2[pl.ds(g * 8 * PAD + row, 8, stride=PAD), :]
                acc = jnp.where(cols // 8 == k, pltpu.roll(val, (k * 8 + 4) % 128, 1), acc)
            up_own[h, g] = acc
        return c

    lax.fori_loop(0, NG, pack, 0)
    edges = [
        remote(up_own, u_r, es.at[0], er.at[0], (left, v)),
        remote(up_own, u_l, es.at[1], er.at[1], (right, v)),
    ]
    for cp in edges:
        cp.start()

    for cp in stat:
        cp.wait_recv()
    stat_e = [
        remote(xm, xr, ss.at[2], sr.at[2], (left, v)),
        remote(xm, xl, ss.at[3], sr.at[3], (right, v)),
    ]
    for cp in stat_e:
        cp.start()

    for cp in edges:
        cp.wait_recv()

    def merge(g, c):
        for h in range(2):
            u_lr[h, g] = jnp.where(cols % 8 < 4, u_l[h, g], u_r[h, g])
        return c

    lax.fori_loop(0, NG, merge, 0)
    fwd = [
        remote(u_lr.at[0], u_h.at[0], us.at[0], ur.at[0], (up, v)),
        remote(u_lr.at[1], u_h.at[1], us.at[1], ur.at[1], (down, v)),
    ]
    for cp in fwd:
        cp.start()
    lax.fori_loop(EARLY, NG, send_halos, 0)

    for cp in stat_e:
        cp.wait_recv()

    lanes = lax.broadcasted_iota(jnp.int32, (16, 128), 1)

    def both(k):
        return xm[k], jnp.where(lanes < 64, xr[k], xl[k])

    wets = both(12)
    for l in range(LEV):
        cxs, cys, czs = both(l), both(4 + l), both(8 + l)
        cps = both(9 + l) if l < 3 else (jnp.zeros((16, 128), F32),) * 2
        for e in range(2):
            cx, cy, cz, cp, wt = cxs[e], cys[e], czs[e], cps[e], wets[e]
            cxn = pltpu.roll(cx, 15, 0)
            cyn = pltpu.roll(jnp.where(lanes == 0, cys[1 - e], cy), 127, 1)
            total = cx + cxn + cy + cyn + cz + cp
            for k, val in enumerate((1.0 - total, cx, cxn, cy, cyn, cz, cp)):
                cf[e, l * NCOEF + k] = wt * val
    for e in range(2):
        cf[e, LEV * NCOEF] = wets[e]

    def spread(r, c):
        for e, dst in ((0, cbm), (1, cbe)):
            for k in range(LEV * NCOEF + 1):
                dst[r, k] = jnp.broadcast_to(cf[e, k, pl.ds(r, 1), :], (8, 128))
        return c

    lax.fori_loop(0, 16, spread, 0)
    for cp in fwd:
        cp.wait_recv()

    last = cols == 127
    first = cols == 0

    def vec_copy(g):
        grp = pl.ds(pl.multiple_of(g * 8, 8), 8)
        return remote(fin.at[pl.ds(w * 16, 16), grp, :], part.at[:, grp, :], vs.at[g], vr.at[g], (t, w))

    def group(g, c):
        for d in range(2):
            halo_copy(g, d).wait_recv()
        def load_row(i, c):
            at = g * 8 * PAD + i
            for src, upk, r in ((om2, u_lr, i + 4), (halo2, u_h, lax.rem(i + 12, 16))):
                pk = upk[i // 4, g]
                for l in range(LEV):
                    k = l * 4 + lax.rem(i, 4)
                    buf[0, r, 2 * l] = cbm[r, KW] * src[pl.ds(at + l * 8, 8, stride=PAD), :]
                    buf[0, r, 2 * l + 1] = cbe[r, KW] * pltpu.roll(pk, lax.rem(252 - k * 8, 128), 1)
            return c

        lax.fori_loop(0, 8, load_row, 0)

        def rows_at(src, dst, rs, final):
            for r in rs:
                mid = [[buf[src, r, 2 * l + e] for e in range(2)] for l in range(LEV)]
                for l in range(LEV):
                    for e in range(1 if final else 2):
                        cb = cbe if e else cbm
                        me, other = mid[l][e], mid[l][1 - e]
                        f_l = pltpu.roll(jnp.where(last, other, me), 1, 1)
                        f_r = pltpu.roll(jnp.where(first, other, me), 127, 1)
                        k = l * NCOEF
                        acc = cb[r, k] * me
                        acc += cb[r, k + 1] * buf[src, r - 1, 2 * l + e] + cb[r, k + 2] * buf[src, r + 1, 2 * l + e]
                        if l > 0:
                            acc += cb[r, k + 5] * mid[l - 1][e]
                        if l < 3:
                            acc += cb[r, k + 6] * mid[l + 1][e]
                        acc += cb[r, k + 3] * f_l + cb[r, k + 4] * f_r
                        if final:
                            fin[l * 8 + r - 4, pl.ds(pl.multiple_of(g * 8, 8), 8), :] = acc
                            out2[pl.ds(g * 256 + l * 8 + r - 4, 8, stride=32), :] = acc
                        else:
                            buf[dst, r, 2 * l + e] = acc

        for p in range(3):
            size = UNROLLS[p]

            def step(i, c, p=p, size=size):
                rows_at(p % 2, 1 - p % 2, [1 + p + size * i + j for j in range(size)], False)
                return c

            lax.fori_loop(0, (14 - 2 * p) // size, step, 0)

        def last_pass(i, c):
            rows_at(1, 0, [4 + 4 * i + j for j in range(4)], True)
            return c

        lax.fori_loop(0, 2, last_pass, 0)
        vec_copy(g).start()
        return c

    lax.fori_loop(0, NG, group, 0)

    def wide(take, i):
        return jnp.concatenate([take(i * GRAM_ROWS + j) for j in range(GRAM_ROWS)], axis=1)

    def weights(i):
        return wide(lambda k: vol_v[pl.ds(lax.rem(k, 8), 1), :], i)

    def own_block(i, acc):
        a = wide(lambda k: fin[k], i)
        return acc + nt_dot(a * weights(i), a)

    g_own = lax.fori_loop(0, 32 // GRAM_ROWS, own_block, jnp.zeros((64, 64), F32))
    for g in range(NG):
        vec_copy(g).wait_recv()

    def cross_block(i, acc):
        mine, theirs = wide(lambda k: fin[v * 16 + k], i), wide(lambda k: part[k], i)
        a = jnp.where(v == 0, mine, theirs)
        b = jnp.where(v == 0, theirs, mine)
        return acc + nt_dot(a * weights(i), b)

    g_cross = lax.fori_loop(0, 16 // GRAM_ROWS, cross_block, jnp.zeros((64, 64), F32))

    def stage(val, red, slot, peers, s, r):
        red[slot] = val
        cps = [remote(red.at[slot], red.at[slot], s.at[j], r.at[j], p) for j, p in enumerate(peers)]
        for cp in cps:
            cp.start()
        for cp in cps:
            cp.wait_recv()
        return cps

    sent = []
    val = jnp.concatenate([g_own, g_cross], axis=1)
    sent += stage(val, red_c, core, [(pair, v)], cs, cr)
    val = red_c[0] + red_c[1]
    sent += stage(val, red_x, px, [(p, v) for p in x_peers], xs, xrs)
    val = (red_x[0] + red_x[1]) + (red_x[2] + red_x[3])
    sent += stage(val, red_y, py, [(p, v) for p in y_peers], ys, yr)
    val = (red_y[0] + red_y[1]) + (red_y[2] + red_y[3])
    sent += stage(val, red_z, 2 * zh + v, [(t, w), (zpair, v), (zpair, w)], zs, zr)
    scale = 1.0 / CELLS
    even = red_z[0] + red_z[2]
    odd = red_z[1] + red_z[3]
    g00 = even[:, :64] * scale
    g11 = odd[:, :64] * scale
    g01 = (even[:, 64:] + odd[:, 64:]) * scale
    gram[pl.ds(0, 64), :] = jnp.concatenate([g00, g01], axis=1)
    gram[pl.ds(64, 64), :] = jnp.concatenate([g01.T, g11], axis=1)

    for cp in sent + stat + stat_e + edges + fwd:
        cp.wait_send()
    for g in range(NG):
        for d in range(2):
            halo_copy(g, d).wait_send()
        vec_copy(g).wait_send()


def factor_kernel(gram, raw, r_out, out, a_ref, hold, sem_in, sem_out):
    fetch = pltpu.make_async_copy(raw, hold, sem_in)
    fetch.start()
    a_ref[...] = gram[...]
    row_id = lax.broadcasted_iota(jnp.int32, (PANEL, 128), 0)
    col_id = lax.broadcasted_iota(jnp.int32, (PANEL, 128), 1)

    def panel(k, c):
        start = pl.multiple_of(k * PANEL, PANEL)
        p = a_ref[pl.ds(start, PANEL), :]
        front = pltpu.roll(p, lax.rem(128 - start, 128), 1)
        cols = [jnp.broadcast_to(front[:, j : j + 1], (PANEL, 128)) for j in range(PANEL)]
        for j in range(PANEL):
            d = cols[j][j : j + 1, :]
            inv = lax.rsqrt(d)
            inv = inv * (1.5 - 0.5 * d * inv * inv)
            below = jnp.where(row_id > j, cols[j] * inv, 0.0)
            u = p[j : j + 1, :] * inv
            p = jnp.where(row_id == j, u, p - below * u)
            for m in range(j + 1, PANEL):
                cols[m] = cols[m] - below * (cols[m][j : j + 1, :] * inv)
        p = jnp.where(col_id >= row_id + start, p, 0.0)
        r_out[pl.ds(start, PANEL), :] = p

        @pl.when(k < 128 // PANEL - 1)
        def _():
            a_ref[...] -= lax.dot_general(
                p, p, (((0,), (0,)), ((), ())), precision=HIGH, preferred_element_type=F32
            )

        return c

    lax.fori_loop(0, 2, panel, 0)
    fetch.wait()
    put = pltpu.make_async_copy(hold, out, sem_out)
    put.start()
    lax.fori_loop(2, 128 // PANEL, panel, 0)
    put.wait()


def factor(gram, raw):
    anys = pl.BlockSpec(memory_space=pl.ANY)
    vmem = pl.BlockSpec(memory_space=pltpu.VMEM)
    return pl.pallas_call(
        factor_kernel,
        out_shape=(jax.ShapeDtypeStruct((128, 128), F32), jax.ShapeDtypeStruct(raw.shape, F32)),
        in_specs=[vmem, anys],
        out_specs=(vmem, anys),
        scratch_shapes=[
            pltpu.VMEM((128, 128), F32), pltpu.VMEM(raw.shape, F32), pltpu.SemaphoreType.DMA, pltpu.SemaphoreType.DMA
        ],
        name="upper_factor",
    )(gram, raw)


def shards(omega, conductance, wet, volume, face_runs):
    vm = lambda *s: pltpu.VMEM(s, F32)
    dma = lambda *s: pltpu.SemaphoreType.DMA(s)
    scratch = [
        vm(64, 5, 8, 128), vm(64, 5, 8, 128), vm(3, 4, 8, 128), pltpu.VMEM((8, 128), jnp.int32), vm(8, 128),
        pltpu.SMEM((1, 4), jnp.int32),
        vm(13, 16, 128), vm(13, 16, 128), vm(13, 16, 128), vm(2, 29, 16, 128),
        vm(16, 29, 8, 128), vm(16, 29, 8, 128),
        vm(2, 8, 8, 128), vm(2, 8, 8, 128), vm(2, 8, 8, 128), vm(2, 8, 8, 128), vm(2, 8, 8, 128),
        vm(2, 16, 8, 8, 128), vm(32, 64, 128), vm(16, 64, 128),
        vm(2, 64, 128), vm(4, 64, 128), vm(4, 64, 128), vm(4, 64, 128),
        dma(5), dma(8, 2), dma(8, 2), dma(4), dma(4), dma(2), dma(2), dma(2), dma(2),
        dma(2), dma(2), dma(8), dma(8), dma(1), dma(1), dma(3), dma(3), dma(3), dma(3), dma(3), dma(3),
    ]
    anys = pl.BlockSpec(memory_space=pl.ANY)
    diffused, gram = pl.pallas_call(
        kernel,
        out_shape=(jax.ShapeDtypeStruct((64, LEV, 8, 128), F32), jax.ShapeDtypeStruct((128, 128), F32)),
        in_specs=[anys] * 5,
        out_specs=(pl.BlockSpec(memory_space=pltpu.VMEM),) * 2,
        scratch_shapes=scratch,
        compiler_params=pltpu.CompilerParams(
            collective_id=0, has_side_effects=True, vmem_limit_bytes=67043328
        ),
        name="range_finder",
    )(omega, conductance, wet, volume, face_runs)
    r_factor, diffused = factor(gram, diffused)
    return (diffused, r_factor)


def solution(mesh):
    in_specs = (
        P("vec", None, "tiles", None),
        P(None, None, "tiles", None),
        P("tiles", None),
        P("tiles", None),
        P("tiles", None),
    )
    out_specs = (P("vec", None, "tiles", None), P())
    return jax.shard_map(shards, mesh=mesh, in_specs=in_specs, out_specs=out_specs, check_vma=False)
```

```python
import functools
import jax
import jax.numpy as jnp
from jax import lax
from jax.sharding import PartitionSpec as P
from jax.experimental import pallas as pl
from jax.experimental.pallas import tpu as pltpu

MESH = pl.DeviceIdType.MESH
F32 = jnp.float32
LEV = 4
NG = 8
NCOEF = 7
UNROLLS = (7, 6, 5)
EARLY = 4
KW = LEV * NCOEF
GRAM_ROWS = 8
PANEL = 16
PAD = 40
CELLS = 4 * 512 * 128
HIGH = lax.Precision.HIGHEST


def did(t, v):
    return {"tiles": t, "vec": v}


def nt_dot(a, b):
    return lax.dot_general(a, b, (((1,), (1,)), ((), ())), precision=HIGH, preferred_element_type=F32)


def kernel(
    om, cond, wet, vol, runs,
    out, gram,
    om_v, halo, cond_v, wet_v, vol_v, runs_s,
    xm, xl, xr, cf, cbm, cbe,
    up_own, u_l, u_r, u_lr, u_h,
    buf, fin, part, out_v,
    red_c, red_x, red_y, red_z,
    lsem, osem, hs, hr, ss, sr, es, er, us, ur, fs, fr, vs, vr, cs, cr, xs, xrs, ys, yr, zs, zr,
):
    t = lax.axis_index("tiles")
    v = lax.axis_index("vec")
    w = 1 - v
    core = lax.rem(t, 2)
    px = lax.rem(t // 2, 4)
    zh = lax.rem(t // 8, 2)
    py = t // 16
    tcol = lax.rem(t, 8)
    base = t - tcol
    up = lax.rem(t + 56, 64)
    down = lax.rem(t + 8, 64)
    left = base + lax.rem(tcol + 7, 8)
    right = base + lax.rem(tcol + 1, 8)
    pair = t + 1 - 2 * core
    zpair = t + 8 - 16 * zh
    x_peers = [t - 2 * px + 2 * lax.rem(px + d, 4) for d in (1, 2, 3)]
    y_peers = [t - 16 * py + 16 * lax.rem(py + d, 4) for d in (1, 2, 3)]

    loads = [
        pltpu.make_async_copy(cond, cond_v, lsem.at[0]),
        pltpu.make_async_copy(wet, wet_v, lsem.at[1]),
        pltpu.make_async_copy(runs, runs_s, lsem.at[2]),
        pltpu.make_async_copy(vol, vol_v, lsem.at[3]),
        pltpu.make_async_copy(om, om_v.at[:, pl.ds(0, LEV)], lsem.at[4]),
    ]
    for cp in loads:
        cp.start()

    barrier = pltpu.get_barrier_semaphore()
    greet = [(up, v), (down, v), (left, v), (right, v)]
    greet += [(p, v) for p in x_peers] + [(p, v) for p in y_peers]
    greet += [(t, w), (zpair, w)]
    for p in greet:
        pl.semaphore_signal(barrier, inc=1, device_id=did(*p), device_id_type=MESH)

    for cp in loads[:3]:
        cp.wait()
    rows = lax.broadcasted_iota(jnp.int32, (8, 128), 0)
    cols = lax.broadcasted_iota(jnp.int32, (8, 128), 1)
    r0, r1, r2, r3 = (runs_s[0, k] for k in range(4))
    closed_x = (rows == 0) & ((cols < r0) | (cols >= r0 + r1))
    closed_y = (cols == 0) & ((rows < r2) | (rows >= r2 + r3))
    own = pl.ds(4, 8)
    for l in range(LEV):
        xm[l, own, :] = jnp.where(closed_x, 0.0, cond_v[0, l])
        xm[4 + l, own, :] = jnp.where(closed_y, 0.0, cond_v[1, l])
        xm[8 + l, own, :] = cond_v[2, l] if l else jnp.zeros((8, 128), F32)
    xm[12, own, :] = wet_v[...].astype(F32)

    pl.semaphore_wait(barrier, len(greet))

    def remote(src, dst, s, r, to):
        return pltpu.make_async_remote_copy(
            src_ref=src, dst_ref=dst, send_sem=s, recv_sem=r, device_id=did(*to), device_id_type=MESH
        )

    stat = [
        remote(xm.at[:, pl.ds(4, 4), :], xm.at[:, pl.ds(12, 4), :], ss.at[0], sr.at[0], (up, v)),
        remote(xm.at[:, pl.ds(8, 4), :], xm.at[:, pl.ds(0, 4), :], ss.at[1], sr.at[1], (down, v)),
    ]
    for cp in stat:
        cp.start()

    def halo_copy(g, d):
        blk = pl.ds(g * 8, 8)
        half = pl.ds(4 * d, 4)
        return remote(
            om.at[blk, :, half, :], halo.at[blk, pl.ds(0, LEV), half, :], hs.at[g, d], hr.at[g, d], (down if d else up, v)
        )

    def send_halos(g, c):
        for d in range(2):
            halo_copy(g, d).start()
        return c

    lax.fori_loop(0, EARLY, send_halos, 0)

    for cp in loads[3:]:
        cp.wait()
    om2 = om_v.reshape(64 * PAD, 128)
    halo2 = halo.reshape(64 * PAD, 128)
    out2 = out_v.reshape(64 * PAD, 128)

    def pack(g, c):
        for h in range(2):
            acc = jnp.zeros((8, 128), F32)
            for k in range(16):
                row = (k // 4) * 8 + 4 * h + k % 4
                val = om2[pl.ds(g * 8 * PAD + row, 8, stride=PAD), :]
                acc = jnp.where(cols // 8 == k, pltpu.roll(val, (k * 8 + 4) % 128, 1), acc)
            up_own[h, g] = acc
        return c

    lax.fori_loop(0, NG, pack, 0)
    edges = [
        remote(up_own, u_r, es.at[0], er.at[0], (left, v)),
        remote(up_own, u_l, es.at[1], er.at[1], (right, v)),
    ]
    for cp in edges:
        cp.start()

    for cp in stat:
        cp.wait_recv()
    stat_e = [
        remote(xm, xr, ss.at[2], sr.at[2], (left, v)),
        remote(xm, xl, ss.at[3], sr.at[3], (right, v)),
    ]
    for cp in stat_e:
        cp.start()

    for cp in edges:
        cp.wait_recv()

    def merge(g, c):
        for h in range(2):
            u_lr[h, g] = jnp.where(cols % 8 < 4, u_l[h, g], u_r[h, g])
        return c

    lax.fori_loop(0, NG, merge, 0)
    fwd = [
        remote(u_lr.at[0], u_h.at[0], us.at[0], ur.at[0], (up, v)),
        remote(u_lr.at[1], u_h.at[1], us.at[1], ur.at[1], (down, v)),
    ]
    for cp in fwd:
        cp.start()
    lax.fori_loop(EARLY, NG, send_halos, 0)

    for cp in stat_e:
        cp.wait_recv()

    lanes = lax.broadcasted_iota(jnp.int32, (16, 128), 1)

    def both(k):
        return xm[k], jnp.where(lanes < 64, xr[k], xl[k])

    wets = both(12)
    for l in range(LEV):
        cxs, cys, czs = both(l), both(4 + l), both(8 + l)
        cps = both(9 + l) if l < 3 else (jnp.zeros((16, 128), F32),) * 2
        for e in range(2):
            cx, cy, cz, cp, wt = cxs[e], cys[e], czs[e], cps[e], wets[e]
            cxn = pltpu.roll(cx, 15, 0)
            cyn = pltpu.roll(jnp.where(lanes == 0, cys[1 - e], cy), 127, 1)
            total = cx + cxn + cy + cyn + cz + cp
            for k, val in enumerate((1.0 - total, cx, cxn, cy, cyn, cz, cp)):
                cf[e, l * NCOEF + k] = wt * val
    for e in range(2):
        cf[e, LEV * NCOEF] = wets[e]

    def spread(r, c):
        for e, dst in ((0, cbm), (1, cbe)):
            for k in range(LEV * NCOEF + 1):
                dst[r, k] = jnp.broadcast_to(cf[e, k, pl.ds(r, 1), :], (8, 128))
        return c

    lax.fori_loop(0, 16, spread, 0)
    for cp in fwd:
        cp.wait_recv()

    last = cols == 127
    first = cols == 0

    def vec_copy(g):
        grp = pl.ds(pl.multiple_of(g * 8, 8), 8)
        return remote(fin.at[pl.ds(w * 16, 16), grp, :], part.at[:, grp, :], vs.at[g], vr.at[g], (t, w))

    def out_copy(g):
        blk = pl.ds(g * 8, 8)
        return pltpu.make_async_copy(out_v.at[blk, pl.ds(0, LEV)], out.at[blk], osem.at[g])

    def group(g, c):
        for d in range(2):
            halo_copy(g, d).wait_recv()
        def load_row(i, c):
            at = g * 8 * PAD + i
            for src, upk, r in ((om2, u_lr, i + 4), (halo2, u_h, lax.rem(i + 12, 16))):
                pk = upk[i // 4, g]
                for l in range(LEV):
                    k = l * 4 + lax.rem(i, 4)
                    buf[0, r, 2 * l] = cbm[r, KW] * src[pl.ds(at + l * 8, 8, stride=PAD), :]
                    buf[0, r, 2 * l + 1] = cbe[r, KW] * pltpu.roll(pk, lax.rem(252 - k * 8, 128), 1)
            return c

        lax.fori_loop(0, 8, load_row, 0)

        def rows_at(src, dst, rs, final):
            for r in rs:
                mid = [[buf[src, r, 2 * l + e] for e in range(2)] for l in range(LEV)]
                for l in range(LEV):
                    for e in range(1 if final else 2):
                        cb = cbe if e else cbm
                        me, other = mid[l][e], mid[l][1 - e]
                        f_l = pltpu.roll(jnp.where(last, other, me), 1, 1)
                        f_r = pltpu.roll(jnp.where(first, other, me), 127, 1)
                        k = l * NCOEF
                        acc = cb[r, k] * me
                        acc += cb[r, k + 1] * buf[src, r - 1, 2 * l + e] + cb[r, k + 2] * buf[src, r + 1, 2 * l + e]
                        if l > 0:
                            acc += cb[r, k + 5] * mid[l - 1][e]
                        if l < 3:
                            acc += cb[r, k + 6] * mid[l + 1][e]
                        acc += cb[r, k + 3] * f_l + cb[r, k + 4] * f_r
                        if final:
                            fin[l * 8 + r - 4, pl.ds(pl.multiple_of(g * 8, 8), 8), :] = acc
                            out2[pl.ds(g * 8 * PAD + l * 8 + r - 4, 8, stride=PAD), :] = acc
                        else:
                            buf[dst, r, 2 * l + e] = acc

        for p in range(3):
            size = UNROLLS[p]

            def step(i, c, p=p, size=size):
                rows_at(p % 2, 1 - p % 2, [1 + p + size * i + j for j in range(size)], False)
                return c

            lax.fori_loop(0, (14 - 2 * p) // size, step, 0)

        def last_pass(i, c):
            rows_at(1, 0, [4 + 4 * i + j for j in range(4)], True)
            return c

        lax.fori_loop(0, 2, last_pass, 0)
        vec_copy(g).start()
        out_copy(g).start()
        return c

    lax.fori_loop(0, NG, group, 0)

    def wide(take, i):
        return jnp.concatenate([take(i * GRAM_ROWS + j) for j in range(GRAM_ROWS)], axis=1)

    def weights(i):
        return wide(lambda k: vol_v[pl.ds(lax.rem(k, 8), 1), :], i)

    def own_block(i, acc):
        a = wide(lambda k: fin[k], i)
        return acc + nt_dot(a * weights(i), a)

    g_own = lax.fori_loop(0, 32 // GRAM_ROWS, own_block, jnp.zeros((64, 64), F32))
    for g in range(NG):
        vec_copy(g).wait_recv()

    def cross_block(i, acc):
        mine, theirs = wide(lambda k: fin[v * 16 + k], i), wide(lambda k: part[k], i)
        a = jnp.where(v == 0, mine, theirs)
        b = jnp.where(v == 0, theirs, mine)
        return acc + nt_dot(a * weights(i), b)

    g_cross = lax.fori_loop(0, 16 // GRAM_ROWS, cross_block, jnp.zeros((64, 64), F32))

    def stage(val, red, slot, peers, s, r):
        red[slot] = val
        cps = [remote(red.at[slot], red.at[slot], s.at[j], r.at[j], p) for j, p in enumerate(peers)]
        for cp in cps:
            cp.start()
        for cp in cps:
            cp.wait_recv()
        return cps

    sent = []
    val = jnp.concatenate([g_own, g_cross], axis=1)
    sent += stage(val, red_c, core, [(pair, v)], cs, cr)
    val = red_c[0] + red_c[1]
    sent += stage(val, red_x, px, [(p, v) for p in x_peers], xs, xrs)
    val = (red_x[0] + red_x[1]) + (red_x[2] + red_x[3])
    sent += stage(val, red_y, py, [(p, v) for p in y_peers], ys, yr)
    val = (red_y[0] + red_y[1]) + (red_y[2] + red_y[3])
    sent += stage(val, red_z, 2 * zh + v, [(t, w), (zpair, v), (zpair, w)], zs, zr)
    scale = 1.0 / CELLS
    even = red_z[0] + red_z[2]
    odd = red_z[1] + red_z[3]
    g00 = even[:, :64] * scale
    g11 = odd[:, :64] * scale
    g01 = (even[:, 64:] + odd[:, 64:]) * scale
    gram[pl.ds(0, 64), :] = jnp.concatenate([g00, g01], axis=1)
    gram[pl.ds(64, 64), :] = jnp.concatenate([g01.T, g11], axis=1)

    for cp in sent + stat + stat_e + edges + fwd:
        cp.wait_send()
    for g in range(NG):
        for d in range(2):
            halo_copy(g, d).wait_send()
        vec_copy(g).wait_send()
        out_copy(g).wait()


def factor_kernel(gram, raw, r_out, out, a_ref, hold, sem_in, sem_out):
    fetch = pltpu.make_async_copy(raw, hold, sem_in)
    fetch.start()
    a_ref[...] = gram[...]
    row_id = lax.broadcasted_iota(jnp.int32, (PANEL, 128), 0)
    col_id = lax.broadcasted_iota(jnp.int32, (PANEL, 128), 1)

    def panel(k, c):
        start = pl.multiple_of(k * PANEL, PANEL)
        p = a_ref[pl.ds(start, PANEL), :]
        front = pltpu.roll(p, lax.rem(128 - start, 128), 1)
        cols = [jnp.broadcast_to(front[:, j : j + 1], (PANEL, 128)) for j in range(PANEL)]
        for j in range(PANEL):
            d = cols[j][j : j + 1, :]
            inv = lax.rsqrt(d)
            inv = inv * (1.5 - 0.5 * d * inv * inv)
            below = jnp.where(row_id > j, cols[j] * inv, 0.0)
            u = p[j : j + 1, :] * inv
            p = jnp.where(row_id == j, u, p - below * u)
            for m in range(j + 1, PANEL):
                cols[m] = cols[m] - below * (cols[m][j : j + 1, :] * inv)
        p = jnp.where(col_id >= row_id + start, p, 0.0)
        r_out[pl.ds(start, PANEL), :] = p

        @pl.when(k < 128 // PANEL - 1)
        def _():
            a_ref[...] -= lax.dot_general(
                p, p, (((0,), (0,)), ((), ())), precision=HIGH, preferred_element_type=F32
            )

        return c

    lax.fori_loop(0, 2, panel, 0)
    fetch.wait()
    put = pltpu.make_async_copy(hold, out, sem_out)
    put.start()
    lax.fori_loop(2, 128 // PANEL, panel, 0)
    put.wait()


def factor(gram, raw):
    anys = pl.BlockSpec(memory_space=pl.ANY)
    vmem = pl.BlockSpec(memory_space=pltpu.VMEM)
    return pl.pallas_call(
        factor_kernel,
        out_shape=(jax.ShapeDtypeStruct((128, 128), F32), jax.ShapeDtypeStruct(raw.shape, F32)),
        in_specs=[vmem, anys],
        out_specs=(vmem, anys),
        scratch_shapes=[
            pltpu.VMEM((128, 128), F32), pltpu.VMEM(raw.shape, F32), pltpu.SemaphoreType.DMA, pltpu.SemaphoreType.DMA
        ],
        name="upper_factor",
    )(gram, raw)


def shards(omega, conductance, wet, volume, face_runs):
    vm = lambda *s: pltpu.VMEM(s, F32)
    dma = lambda *s: pltpu.SemaphoreType.DMA(s)
    scratch = [
        vm(64, 5, 8, 128), vm(64, 5, 8, 128), vm(3, 4, 8, 128), pltpu.VMEM((8, 128), jnp.int32), vm(8, 128),
        pltpu.SMEM((1, 4), jnp.int32),
        vm(13, 16, 128), vm(13, 16, 128), vm(13, 16, 128), vm(2, 29, 16, 128),
        vm(16, 29, 8, 128), vm(16, 29, 8, 128),
        vm(2, 8, 8, 128), vm(2, 8, 8, 128), vm(2, 8, 8, 128), vm(2, 8, 8, 128), vm(2, 8, 8, 128),
        vm(2, 16, 8, 8, 128), vm(32, 64, 128), vm(16, 64, 128), vm(64, 5, 8, 128),
        vm(2, 64, 128), vm(4, 64, 128), vm(4, 64, 128), vm(4, 64, 128),
        dma(5), dma(8), dma(8, 2), dma(8, 2), dma(4), dma(4), dma(2), dma(2), dma(2), dma(2),
        dma(2), dma(2), dma(8), dma(8), dma(1), dma(1), dma(3), dma(3), dma(3), dma(3), dma(3), dma(3),
    ]
    anys = pl.BlockSpec(memory_space=pl.ANY)
    diffused, gram = pl.pallas_call(
        kernel,
        out_shape=(jax.ShapeDtypeStruct((64, LEV, 8, 128), F32), jax.ShapeDtypeStruct((128, 128), F32)),
        in_specs=[anys] * 5,
        out_specs=(anys, pl.BlockSpec(memory_space=pltpu.VMEM)),
        scratch_shapes=scratch,
        compiler_params=pltpu.CompilerParams(
            collective_id=0, has_side_effects=True, vmem_limit_bytes=67043328
        ),
        name="range_finder",
    )(omega, conductance, wet, volume, face_runs)
    r_factor, diffused = factor(gram, diffused)
    return (diffused, r_factor)


def solution(mesh):
    in_specs = (
        P("vec", None, "tiles", None),
        P(None, None, "tiles", None),
        P("tiles", None),
        P("tiles", None),
        P("tiles", None),
    )
    out_specs = (P("vec", None, "tiles", None), P())
    return jax.shard_map(shards, mesh=mesh, in_specs=in_specs, out_specs=out_specs, check_vma=False)
```

```python
import functools
import jax
import jax.numpy as jnp
from jax import lax
from jax.sharding import PartitionSpec as P
from jax.experimental import pallas as pl
from jax.experimental.pallas import tpu as pltpu

MESH = pl.DeviceIdType.MESH
F32 = jnp.float32
LEV = 4
NG = 8
NCOEF = 7
UNROLLS = (7, 6, 5)
EARLY = 4
KW = LEV * NCOEF
GRAM_ROWS = 8
PANEL = 16
PAD = 40
CELLS = 4 * 512 * 128
HIGH = lax.Precision.HIGHEST


def did(t, v):
    return {"tiles": t, "vec": v}


def nt_dot(a, b):
    return lax.dot_general(a, b, (((1,), (1,)), ((), ())), precision=HIGH, preferred_element_type=F32)


def kernel(
    om, cond, wet, vol, runs,
    out, gram,
    om_v, halo, cond_v, wet_v, vol_v, runs_s,
    xm, xl, xr, cf, cbm, cbe,
    up_own, u_l, u_r, u_lr, u_h,
    buf, fin, part, out_v,
    red_c, red_x, red_y, red_z,
    lsem, osem, hs, hr, ss, sr, es, er, us, ur, fs, fr, vs, vr, cs, cr, xs, xrs, ys, yr, zs, zr,
):
    t = lax.axis_index("tiles")
    v = lax.axis_index("vec")
    w = 1 - v
    core = lax.rem(t, 2)
    px = lax.rem(t // 2, 4)
    zh = lax.rem(t // 8, 2)
    py = t // 16
    tcol = lax.rem(t, 8)
    base = t - tcol
    up = lax.rem(t + 56, 64)
    down = lax.rem(t + 8, 64)
    left = base + lax.rem(tcol + 7, 8)
    right = base + lax.rem(tcol + 1, 8)
    pair = t + 1 - 2 * core
    zpair = t + 8 - 16 * zh
    x_peers = [t - 2 * px + 2 * lax.rem(px + d, 4) for d in (1, 2, 3)]
    y_peers = [t - 16 * py + 16 * lax.rem(py + d, 4) for d in (1, 2, 3)]

    loads = [
        pltpu.make_async_copy(cond, cond_v, lsem.at[0]),
        pltpu.make_async_copy(wet, wet_v, lsem.at[1]),
        pltpu.make_async_copy(runs, runs_s, lsem.at[2]),
        pltpu.make_async_copy(vol, vol_v, lsem.at[3]),
        pltpu.make_async_copy(om, om_v.at[:, pl.ds(0, LEV)], lsem.at[4]),
    ]
    for cp in loads:
        cp.start()

    barrier = pltpu.get_barrier_semaphore()
    greet = [(up, v), (down, v), (left, v), (right, v)]
    greet += [(p, v) for p in x_peers] + [(p, v) for p in y_peers]
    greet += [(t, w), (zpair, w)]
    for p in greet:
        pl.semaphore_signal(barrier, inc=1, device_id=did(*p), device_id_type=MESH)

    for cp in loads[:3]:
        cp.wait()
    rows = lax.broadcasted_iota(jnp.int32, (8, 128), 0)
    cols = lax.broadcasted_iota(jnp.int32, (8, 128), 1)
    r0, r1, r2, r3 = (runs_s[0, k] for k in range(4))
    closed_x = (rows == 0) & ((cols < r0) | (cols >= r0 + r1))
    closed_y = (cols == 0) & ((rows < r2) | (rows >= r2 + r3))
    own = pl.ds(4, 8)
    for l in range(LEV):
        xm[l, own, :] = jnp.where(closed_x, 0.0, cond_v[0, l])
        xm[4 + l, own, :] = jnp.where(closed_y, 0.0, cond_v[1, l])
        xm[8 + l, own, :] = cond_v[2, l] if l else jnp.zeros((8, 128), F32)
    xm[12, own, :] = wet_v[...].astype(F32)

    pl.semaphore_wait(barrier, len(greet))

    def remote(src, dst, s, r, to):
        return pltpu.make_async_remote_copy(
            src_ref=src, dst_ref=dst, send_sem=s, recv_sem=r, device_id=did(*to), device_id_type=MESH
        )

    stat = [
        remote(xm.at[:, pl.ds(4, 4), :], xm.at[:, pl.ds(12, 4), :], ss.at[0], sr.at[0], (up, v)),
        remote(xm.at[:, pl.ds(8, 4), :], xm.at[:, pl.ds(0, 4), :], ss.at[1], sr.at[1], (down, v)),
    ]
    for cp in stat:
        cp.start()

    def halo_copy(g, d):
        blk = pl.ds(g * 8, 8)
        half = pl.ds(4 * d, 4)
        return remote(
            om.at[blk, :, half, :], halo.at[blk, pl.ds(0, LEV), half, :], hs.at[g, d], hr.at[g, d], (down if d else up, v)
        )

    def send_halos(g, c):
        for d in range(2):
            halo_copy(g, d).start()
        return c

    lax.fori_loop(0, EARLY, send_halos, 0)

    for cp in loads[3:]:
        cp.wait()
    om2 = om_v.reshape(64 * PAD, 128)
    halo2 = halo.reshape(64 * PAD, 128)
    out2 = out_v.reshape(64 * PAD, 128)

    def pack(g, c):
        for h in range(2):
            acc = jnp.zeros((8, 128), F32)
            for k in range(16):
                row = (k // 4) * 8 + 4 * h + k % 4
                val = om2[pl.ds(g * 8 * PAD + row, 8, stride=PAD), :]
                acc = jnp.where(cols // 8 == k, pltpu.roll(val, (k * 8 + 4) % 128, 1), acc)
            up_own[h, g] = acc
        return c

    lax.fori_loop(0, NG, pack, 0)
    edges = [
        remote(up_own, u_r, es.at[0], er.at[0], (left, v)),
        remote(up_own, u_l, es.at[1], er.at[1], (right, v)),
    ]
    for cp in edges:
        cp.start()

    for cp in stat:
        cp.wait_recv()
    stat_e = [
        remote(xm, xr, ss.at[2], sr.at[2], (left, v)),
        remote(xm, xl, ss.at[3], sr.at[3], (right, v)),
    ]
    for cp in stat_e:
        cp.start()

    for cp in edges:
        cp.wait_recv()

    def merge(g, c):
        for h in range(2):
            u_lr[h, g] = jnp.where(cols % 8 < 4, u_l[h, g], u_r[h, g])
        return c

    lax.fori_loop(0, NG, merge, 0)
    fwd = [
        remote(u_lr.at[0], u_h.at[0], us.at[0], ur.at[0], (up, v)),
        remote(u_lr.at[1], u_h.at[1], us.at[1], ur.at[1], (down, v)),
    ]
    for cp in fwd:
        cp.start()
    lax.fori_loop(EARLY, NG, send_halos, 0)

    for cp in stat_e:
        cp.wait_recv()

    lanes = lax.broadcasted_iota(jnp.int32, (16, 128), 1)

    def both(k):
        return xm[k], jnp.where(lanes < 64, xr[k], xl[k])

    wets = both(12)
    for l in range(LEV):
        cxs, cys, czs = both(l), both(4 + l), both(8 + l)
        cps = both(9 + l) if l < 3 else (jnp.zeros((16, 128), F32),) * 2
        for e in range(2):
            cx, cy, cz, cp, wt = cxs[e], cys[e], czs[e], cps[e], wets[e]
            cxn = pltpu.roll(cx, 15, 0)
            cyn = pltpu.roll(jnp.where(lanes == 0, cys[1 - e], cy), 127, 1)
            total = cx + cxn + cy + cyn + cz + cp
            for k, val in enumerate((1.0 - total, cx, cxn, cy, cyn, cz, cp)):
                cf[e, l * NCOEF + k] = wt * val
    for e in range(2):
        cf[e, LEV * NCOEF] = wets[e]

    def spread(r, c):
        for e, dst in ((0, cbm), (1, cbe)):
            for k in range(LEV * NCOEF + 1):
                dst[r, k] = jnp.broadcast_to(cf[e, k, pl.ds(r, 1), :], (8, 128))
        return c

    lax.fori_loop(0, 16, spread, 0)
    for cp in fwd:
        cp.wait_recv()

    last = cols == 127
    first = cols == 0

    def vec_copy(g):
        grp = pl.ds(pl.multiple_of(g * 8, 8), 8)
        return remote(fin.at[pl.ds(w * 16, 16), grp, :], part.at[:, grp, :], vs.at[g], vr.at[g], (t, w))

    def out_copy(g):
        blk = pl.ds(g * 8, 8)
        return pltpu.make_async_copy(out_v.at[blk, pl.ds(0, LEV)], out.at[blk], osem.at[g])

    def group(g, c):
        for d in range(2):
            halo_copy(g, d).wait_recv()
        def load_row(i, c):
            at = g * 8 * PAD + i
            for src, upk, r in ((om2, u_lr, i + 4), (halo2, u_h, lax.rem(i + 12, 16))):
                pk = upk[i // 4, g]
                for l in range(LEV):
                    k = l * 4 + lax.rem(i, 4)
                    buf[0, r, 2 * l] = cbm[r, KW] * src[pl.ds(at + l * 8, 8, stride=PAD), :]
                    buf[0, r, 2 * l + 1] = cbe[r, KW] * pltpu.roll(pk, lax.rem(252 - k * 8, 128), 1)
            return c

        lax.fori_loop(0, 8, load_row, 0, unroll=2)

        def rows_at(src, dst, rs, final):
            for r in rs:
                mid = [[buf[src, r, 2 * l + e] for e in range(2)] for l in range(LEV)]
                for l in range(LEV):
                    for e in range(1 if final else 2):
                        cb = cbe if e else cbm
                        me, other = mid[l][e], mid[l][1 - e]
                        f_l = pltpu.roll(jnp.where(last, other, me), 1, 1)
                        f_r = pltpu.roll(jnp.where(first, other, me), 127, 1)
                        k = l * NCOEF
                        acc = cb[r, k] * me
                        acc += cb[r, k + 1] * buf[src, r - 1, 2 * l + e] + cb[r, k + 2] * buf[src, r + 1, 2 * l + e]
                        if l > 0:
                            acc += cb[r, k + 5] * mid[l - 1][e]
                        if l < 3:
                            acc += cb[r, k + 6] * mid[l + 1][e]
                        acc += cb[r, k + 3] * f_l + cb[r, k + 4] * f_r
                        if final:
                            fin[l * 8 + r - 4, pl.ds(pl.multiple_of(g * 8, 8), 8), :] = acc
                            out2[pl.ds(g * 8 * PAD + l * 8 + r - 4, 8, stride=PAD), :] = acc
                        else:
                            buf[dst, r, 2 * l + e] = acc

        for p in range(3):
            size = UNROLLS[p]

            def step(i, c, p=p, size=size):
                rows_at(p % 2, 1 - p % 2, [1 + p + size * i + j for j in range(size)], False)
                return c

            lax.fori_loop(0, (14 - 2 * p) // size, step, 0)

        def last_pass(i, c):
            rows_at(1, 0, [4 + 8 * i + j for j in range(8)], True)
            return c

        lax.fori_loop(0, 1, last_pass, 0)
        vec_copy(g).start()
        out_copy(g).start()
        return c

    lax.fori_loop(0, NG, group, 0)

    def wide(take, i):
        return jnp.concatenate([take(i * GRAM_ROWS + j) for j in range(GRAM_ROWS)], axis=1)

    def weights(i):
        return wide(lambda k: vol_v[pl.ds(lax.rem(k, 8), 1), :], i)

    def own_block(i, acc):
        a = wide(lambda k: fin[k], i)
        return acc + nt_dot(a * weights(i), a)

    g_own = lax.fori_loop(0, 32 // GRAM_ROWS, own_block, jnp.zeros((64, 64), F32))
    for g in range(NG):
        vec_copy(g).wait_recv()

    def cross_block(i, acc):
        mine, theirs = wide(lambda k: fin[v * 16 + k], i), wide(lambda k: part[k], i)
        a = jnp.where(v == 0, mine, theirs)
        b = jnp.where(v == 0, theirs, mine)
        return acc + nt_dot(a * weights(i), b)

    g_cross = lax.fori_loop(0, 16 // GRAM_ROWS, cross_block, jnp.zeros((64, 64), F32))

    def stage(val, red, slot, peers, s, r):
        red[slot] = val
        cps = [remote(red.at[slot], red.at[slot], s.at[j], r.at[j], p) for j, p in enumerate(peers)]
        for cp in cps:
            cp.start()
        for cp in cps:
            cp.wait_recv()
        return cps

    sent = []
    val = jnp.concatenate([g_own, g_cross], axis=1)
    sent += stage(val, red_c, core, [(pair, v)], cs, cr)
    val = red_c[0] + red_c[1]
    sent += stage(val, red_x, px, [(p, v) for p in x_peers], xs, xrs)
    val = (red_x[0] + red_x[1]) + (red_x[2] + red_x[3])
    sent += stage(val, red_y, py, [(p, v) for p in y_peers], ys, yr)
    val = (red_y[0] + red_y[1]) + (red_y[2] + red_y[3])
    sent += stage(val, red_z, 2 * zh + v, [(t, w), (zpair, v), (zpair, w)], zs, zr)
    scale = 1.0 / CELLS
    even = red_z[0] + red_z[2]
    odd = red_z[1] + red_z[3]
    g00 = even[:, :64] * scale
    g11 = odd[:, :64] * scale
    g01 = (even[:, 64:] + odd[:, 64:]) * scale
    gram[pl.ds(0, 64), :] = jnp.concatenate([g00, g01], axis=1)
    gram[pl.ds(64, 64), :] = jnp.concatenate([g01.T, g11], axis=1)

    for cp in sent + stat + stat_e + edges + fwd:
        cp.wait_send()
    for g in range(NG):
        for d in range(2):
            halo_copy(g, d).wait_send()
        vec_copy(g).wait_send()
        out_copy(g).wait()


def factor_kernel(gram, raw, r_out, out, a_ref, hold, sem_in, sem_out):
    fetch = pltpu.make_async_copy(raw, hold, sem_in)
    fetch.start()
    a_ref[...] = gram[...]
    row_id = lax.broadcasted_iota(jnp.int32, (PANEL, 128), 0)
    col_id = lax.broadcasted_iota(jnp.int32, (PANEL, 128), 1)

    def panel(k, c):
        start = pl.multiple_of(k * PANEL, PANEL)
        p = a_ref[pl.ds(start, PANEL), :]
        front = pltpu.roll(p, lax.rem(128 - start, 128), 1)
        cols = [jnp.broadcast_to(front[:, j : j + 1], (PANEL, 128)) for j in range(PANEL)]
        for j in range(PANEL):
            d = cols[j][j : j + 1, :]
            inv = lax.rsqrt(d)
            inv = inv * (1.5 - 0.5 * d * inv * inv)
            below = jnp.where(row_id > j, cols[j] * inv, 0.0)
            u = p[j : j + 1, :] * inv
            p = jnp.where(row_id == j, u, p - below * u)
            for m in range(j + 1, PANEL):
                cols[m] = cols[m] - below * (cols[m][j : j + 1, :] * inv)
        p = jnp.where(col_id >= row_id + start, p, 0.0)
        r_out[pl.ds(start, PANEL), :] = p

        @pl.when(k < 128 // PANEL - 1)
        def _():
            a_ref[...] -= lax.dot_general(
                p, p, (((0,), (0,)), ((), ())), precision=HIGH, preferred_element_type=F32
            )

        return c

    lax.fori_loop(0, 2, panel, 0)
    fetch.wait()
    put = pltpu.make_async_copy(hold, out, sem_out)
    put.start()
    lax.fori_loop(2, 128 // PANEL, panel, 0)
    put.wait()


def factor(gram, raw):
    anys = pl.BlockSpec(memory_space=pl.ANY)
    vmem = pl.BlockSpec(memory_space=pltpu.VMEM)
    return pl.pallas_call(
        factor_kernel,
        out_shape=(jax.ShapeDtypeStruct((128, 128), F32), jax.ShapeDtypeStruct(raw.shape, F32)),
        in_specs=[vmem, anys],
        out_specs=(vmem, anys),
        scratch_shapes=[
            pltpu.VMEM((128, 128), F32), pltpu.VMEM(raw.shape, F32), pltpu.SemaphoreType.DMA, pltpu.SemaphoreType.DMA
        ],
        name="upper_factor",
    )(gram, raw)


def shards(omega, conductance, wet, volume, face_runs):
    vm = lambda *s: pltpu.VMEM(s, F32)
    dma = lambda *s: pltpu.SemaphoreType.DMA(s)
    scratch = [
        vm(64, 5, 8, 128), vm(64, 5, 8, 128), vm(3, 4, 8, 128), pltpu.VMEM((8, 128), jnp.int32), vm(8, 128),
        pltpu.SMEM((1, 4), jnp.int32),
        vm(13, 16, 128), vm(13, 16, 128), vm(13, 16, 128), vm(2, 29, 16, 128),
        vm(16, 29, 8, 128), vm(16, 29, 8, 128),
        vm(2, 8, 8, 128), vm(2, 8, 8, 128), vm(2, 8, 8, 128), vm(2, 8, 8, 128), vm(2, 8, 8, 128),
        vm(2, 16, 8, 8, 128), vm(32, 64, 128), vm(16, 64, 128), vm(64, 5, 8, 128),
        vm(2, 64, 128), vm(4, 64, 128), vm(4, 64, 128), vm(4, 64, 128),
        dma(5), dma(8), dma(8, 2), dma(8, 2), dma(4), dma(4), dma(2), dma(2), dma(2), dma(2),
        dma(2), dma(2), dma(8), dma(8), dma(1), dma(1), dma(3), dma(3), dma(3), dma(3), dma(3), dma(3),
    ]
    anys = pl.BlockSpec(memory_space=pl.ANY)
    diffused, gram = pl.pallas_call(
        kernel,
        out_shape=(jax.ShapeDtypeStruct((64, LEV, 8, 128), F32), jax.ShapeDtypeStruct((128, 128), F32)),
        in_specs=[anys] * 5,
        out_specs=(anys, pl.BlockSpec(memory_space=pltpu.VMEM)),
        scratch_shapes=scratch,
        compiler_params=pltpu.CompilerParams(
            collective_id=0, has_side_effects=True, vmem_limit_bytes=67043328
        ),
        name="range_finder",
    )(omega, conductance, wet, volume, face_runs)
    r_factor, diffused = factor(gram, diffused)
    return (diffused, r_factor)


def solution(mesh):
    in_specs = (
        P("vec", None, "tiles", None),
        P(None, None, "tiles", None),
        P("tiles", None),
        P("tiles", None),
        P("tiles", None),
    )
    out_specs = (P("vec", None, "tiles", None), P())
    return jax.shard_map(shards, mesh=mesh, in_specs=in_specs, out_specs=out_specs, check_vma=False)
```
